512 devices in a mesh: seq: 8 (over z), exp: 64 (over x, y, core).
Axes of the slice: x: 4, y: 8, z: 8, core: 2. Of those that a mesh axis runs over, the one named last changes fastest.
Arguments:
- tokens: bfloat16 [65536, 4096], P(('seq', 'exp')), may hold values from -6 to 6
- cotangent: bfloat16 [65536, 4096], P(('seq', 'exp')), may hold values from -3 to 3
- factors: bfloat16 [64, 3, 4, 1024, 128], P('exp', None, None, 'seq'), may hold values from -0.09375 to 0.09375
- mix: float32 [64, 3, 4, 4, 4], P('exp'), may hold values from -3 to 3
- selection: int32 [64, 16, 64], P('exp', 'seq'), may hold values from 0 to 4095, as said below
- scores: int32 [64, 16, 64], P('exp', 'seq'), may hold values from -192 to 191
Outputs:
- token_grad: bfloat16 [65536, 4096], P(('seq', 'exp'))
- factor_grad: float32 [64, 3, 4, 1024, 128], P('exp', None, None, 'seq')
- mix_grad: float32 [64, 3, 4, 4, 4], P('exp')
- gate_grad: float32 [64, 16, 64], P('exp', 'seq')
The draws below stay inside these ranges and needn't reach their ends.
Inputs may be any that keep to these rules, and one draw needn't show every extreme that they name: `selection`: for every expert and block the 64 positions are distinct and ascending; at most 3 of them lie among the 128 positions of one device (aligned runs of 128), and for every expert and block some device holds exactly 3 of them.
All inputs are finite; a program needn't handle non-finite values.
Results may differ from the reference program's by a relative error of at most 0.015.
Values may be sent and summed in bfloat16 or wider, within the bound.
A program may use at most 64 MiB of HBM per device.

```python
import jax
import jax.numpy as jnp
from jax import lax

D = 4096
FF = 512
NPHM = 4
C = 64
TOK_DEV = 128
EXPERTS = 64
BLOCK = 4096
CAP = 3
GROUPS = 8
BLOCKS = 16
ROWS = 128
TOKENS = 65536


def draw_selection(key, part):
    key_rank = jax.random.fold_in(key, 11)
    key_favour = jax.random.fold_in(key, 12)
    key_forced = jax.random.fold_in(key, 13)
    key_jitter = jax.random.fold_in(key, 14)
    owner_total = BLOCK // TOK_DEV
    rank_keys = jax.random.randint(key_rank, (EXPERTS, BLOCKS, owner_total, TOK_DEV), 0, 1 << 20)
    local_idx = jnp.arange(TOK_DEV, dtype=jnp.int32)
    rank_keys = rank_keys * TOK_DEV + local_idx
    run_order = jnp.argsort(jnp.argsort(rank_keys, axis=-1), axis=-1)
    allowed = run_order < CAP
    favour = jax.random.randint(key_favour, (1, BLOCKS, owner_total, 1), 0, 4)
    forced_owner = jax.random.randint(key_forced, (EXPERTS, BLOCKS, 1, 1), 0, owner_total)
    jitter = jax.random.randint(key_jitter, (EXPERTS, BLOCKS, owner_total, TOK_DEV), 0, 1024)
    owner_ids = jnp.arange(owner_total, dtype=jnp.int32)[None, None, :, None]
    priority = 1 + favour * 1024 + jitter + (owner_ids == forced_owner).astype(jnp.int32) * 8192
    priority = jnp.where(allowed, priority, 0)
    ranked = priority.reshape(EXPERTS, BLOCKS, BLOCK) * BLOCK + jnp.arange(BLOCK, dtype=jnp.int32)
    ignored, picked = lax.top_k(ranked, C)
    return jnp.sort(picked, axis=-1).astype(jnp.int32)


def set_ends(values, rng, least, top_value):
    shape = values.shape
    place = [jax.random.randint(jax.random.fold_in(rng, axis), (), 0, shape[axis]) for axis in range(len(shape))]
    values = values.at[tuple(place)].set(least)
    longest = shape.index(max(shape))
    place[longest] = (place[longest] + 1) % shape[longest]
    return values.at[tuple(place)].set(top_value)


def block_scale(own_key, extent, cuts, low, high):
    loudness, own = 1.0, jax.random.fold_in(own_key, 6)
    for position, parts in cuts:
        steps = jnp.exp(jax.random.uniform(jax.random.fold_in(own, position), (parts,), jnp.float32, low / len(cuts), high / len(cuts)))
        loudness = loudness * jnp.repeat(steps, extent[position] // parts).reshape([-1 if axis == position else 1 for axis in range(len(extent))])
    return loudness


def gaussian(key, dims, width, most, shards=(), held_as=jnp.bfloat16):
    factor_of = block_scale(key, dims, shards, -0.22, 0.18) if shards else 1.0
    entries = jax.random.normal(key, dims, jnp.float32) * width * factor_of
    return jnp.minimum(jnp.maximum(entries, -most), most).astype(held_as)


def setup_inputs(seed: int = 0) -> dict:
    key_list = jax.random.split(jax.random.key(seed), 7)
    return {
        "tokens": gaussian(key_list[0], (TOKENS, D), 1.0, 6.0, ((0, 512),)),
        "cotangent": gaussian(key_list[1], (TOKENS, D), 0.5, 3.0, ((0, 512),)),
        "factors": gaussian(key_list[2], (EXPERTS, 3, NPHM, D // NPHM, FF // NPHM), D ** -0.5, 0.09375, ((0, 64), (3, 8))),
        "mix": gaussian(key_list[3], (EXPERTS, 3, NPHM, NPHM, NPHM), 0.5, 3.0, ((0, 64),), jnp.float32),
        "selection": draw_selection(jax.random.fold_in(key_list[6], 71), 0),
        "scores": set_ends(jax.random.randint(key_list[5], (EXPERTS, BLOCKS, C), -192, 192), jax.random.fold_in(key_list[5], 1), -192, 191).astype(jnp.int32),
    }


PRECISE = lax.Precision.HIGHEST


def expand(mixing, factor_set):
    shape_set = factor_set.shape
    expanded = jnp.einsum("iab,ipq->apbq", mixing, factor_set.astype(jnp.float32), precision=PRECISE)
    return expanded.reshape(shape_set[0] * shape_set[1], shape_set[0] * shape_set[2])


def project(mixing, factor_set, kernel_grad):
    shape_set = factor_set.shape
    block_view = kernel_grad.reshape(shape_set[0], shape_set[1], shape_set[0], shape_set[2])
    factor_out = jnp.einsum("iab,apbq->ipq", mixing, block_view, precision=PRECISE)
    mixing_out = jnp.einsum("apbq,ipq->iab", block_view, factor_set.astype(jnp.float32), precision=PRECISE)
    return factor_out, mixing_out


def silu_parts(preact):
    sigmoid_val = jax.nn.sigmoid(preact)
    return preact * sigmoid_val, sigmoid_val + preact * sigmoid_val * (1.0 - sigmoid_val)


def contract(left, right):
    return lax.dot_general(left, right, (((0,), (0,)), ((), ())), preferred_element_type=jnp.float32)


def transposed(left, kernel):
    return lax.dot_general(left, kernel, (((1,), (1,)), ((), ())), preferred_element_type=jnp.float32)


def expert_core(sel_rows, sel_grads, gate_val, kernels):
    pre_gate = jnp.dot(sel_rows, kernels[0], preferred_element_type=jnp.float32)
    pre_up = jnp.dot(sel_rows, kernels[1], preferred_element_type=jnp.float32)
    gate_act, gate_slope = silu_parts(pre_gate)
    hidden = (gate_act * pre_up).astype(jnp.bfloat16)
    expert_out = transposed(hidden, kernels[2])
    gate_in = jnp.sum(sel_grads.astype(jnp.float32) * expert_out, axis=1)
    gate_grad = gate_in * gate_val * (1.0 - gate_val)
    out_grad = (gate_val[:, None] * sel_grads.astype(jnp.float32)).astype(jnp.bfloat16)
    hidden_grad = jnp.dot(out_grad, kernels[2], preferred_element_type=jnp.float32)
    gate_pre = (hidden_grad * pre_up * gate_slope).astype(jnp.bfloat16)
    up_pre = (hidden_grad * gate_act).astype(jnp.bfloat16)
    row_grad = (transposed(gate_pre, kernels[0]) + transposed(up_pre, kernels[1])).astype(jnp.bfloat16)
    return gate_grad, row_grad, gate_pre, up_pre, out_grad, hidden


def reference(tokens, cotangent, factors, mix, selection, scores):
    def one_expert(running, inputs):
        chosen, score_set, factor_e, mix_e = inputs
        kernels = [expand(mix_e[number], factor_e[number]).astype(jnp.bfloat16) for number in range(3)]
        token_index = (jnp.arange(BLOCKS, dtype=jnp.int32)[:, None] * BLOCK + chosen).reshape(-1).astype(jnp.int32)
        sel_rows = jnp.take(tokens, token_index, axis=0)
        sel_grads = jnp.take(cotangent, token_index, axis=0)
        gate_val = jax.nn.sigmoid(score_set.reshape(-1).astype(jnp.float32) / 64.0)
        gate_grad, row_grad, gate_pre, up_pre, out_grad, hidden = expert_core(sel_rows, sel_grads, gate_val, kernels)
        running = running.at[token_index].add(row_grad.astype(jnp.float32))

        def group_part(pieces):
            rows_g, gate_g, up_g, out_g, hidden_g = pieces
            kernel_grads = [contract(rows_g, gate_g), contract(rows_g, up_g), contract(out_g, hidden_g)]
            projected = [project(mix_e[number], factor_e[number], kernel_grads[number]) for number in range(3)]
            factor_part = jnp.stack([item[0] for item in projected]).astype(jnp.bfloat16)
            mix_part = jnp.stack([item[1] for item in projected])
            return factor_part, mix_part

        grouped = tuple(array.reshape(GROUPS, ROWS, array.shape[-1]) for array in (sel_rows, gate_pre, up_pre, out_grad, hidden))
        factor_parts, mix_parts = lax.map(group_part, grouped)
        factor_parts = lax.optimization_barrier(factor_parts)
        factor_grad = jnp.sum(factor_parts.astype(jnp.float32), axis=0)
        mix_grad = jnp.sum(mix_parts, axis=0)
        return running, (factor_grad, mix_grad, gate_grad.reshape(BLOCKS, C))

    initial = jnp.zeros((TOKENS, D), jnp.float32)
    token_grad, stacked = lax.scan(one_expert, initial, (selection, scores, factors, mix))
    return token_grad.astype(jnp.bfloat16), stacked[0], stacked[1], stacked[2]
```

```python
import jax
import jax.numpy as jnp
from jax import lax
from jax.experimental import pallas as pl
from jax.experimental.pallas import tpu as pltpu
from jax.sharding import PartitionSpec as P

MESH = pl.DeviceIdType.MESH
BF = jnp.bfloat16
F32 = jnp.float32
I32 = jnp.int32
FWD = 8
RET = 4
AHEAD = 3


def dot(a, b):
    return lax.dot_general(a, b, (((1,), (0,)), ((), ())), preferred_element_type=F32)


def dot_nt(a, b):
    return lax.dot_general(a, b, (((1,), (1,)), ((), ())), preferred_element_type=F32)


def dot_tn(a, b):
    return lax.dot_general(a, b, (((0,), (0,)), ((), ())), preferred_element_type=F32)


def iota(shape, dim):
    return lax.broadcasted_iota(I32, shape, dim)


def each(n, body):
    lax.fori_loop(0, n, lambda d, carry: (body(d), carry)[1], 0)


def kernel(
    tok, cot, fac, mix, ints, tok_out, fac_out, mix_out, gate_out,
    selx, sely, pick, pick_t, chose, chose_t, perm,
    send1, recv1, send2, recv2, send3, recv3, send4, recv4,
    fbuf, xs, ybuf, ubuf, ends, gates, ggs, mdrow, mixbuf,
    plus_s, plus_r, minus_s, minus_r,
    selx_sem, sely_sem, y_sem, x_sem, bx_sem, by_sem, agp_sem, agm_sem, rsp_sem, rsm_sem, mix_sem,
):
    me = lax.axis_index("exp")
    z = lax.axis_index("seq")
    core, y, x = lax.rem(me, 2), lax.rem(me // 2, 8), me // 16
    g = x * 2 + core

    def at_y(d):
        return {"exp": (x * 8 + lax.rem(y + d + 1, 8)) * 2 + core, "seq": z}

    def at_g(d):
        o = lax.rem(g + d + 1, 8)
        return {"exp": ((o // 2) * 8 + y) * 2 + lax.rem(o, 2), "seq": z}

    def at_z(d):
        return {"exp": me, "seq": lax.rem(z + d + 1, 8)}

    def remote(src, dst, sems, where):
        return pltpu.make_async_remote_copy(
            src_ref=src, dst_ref=dst, send_sem=sems[0], recv_sem=sems[1],
            device_id=where, device_id_type=MESH,
        )

    barrier = pltpu.get_barrier_semaphore()
    for place in (at_g, at_y, at_z):
        each(7, lambda d, place=place: pl.semaphore_signal(barrier, inc=1, device_id=place(d), device_id_type=MESH))
    pl.semaphore_wait(barrier, 21)

    def selx_copy(d):
        return remote(selx.at[g], selx.at[g], (selx_sem.at[0, d], selx_sem.at[1, d]), at_g(d))

    selx[g] = ints[0]
    each(7, lambda d: selx_copy(d).start())

    for m in range(3):
        for i in range(4):
            fbuf[z, m, :, i * 128 : (i + 1) * 128] = fac[0, m, i]

    def agp_copy(s):
        slot = lax.rem(z - s + 8, 8)
        return remote(fbuf.at[slot], fbuf.at[slot], (agp_sem.at[0, s], agp_sem.at[1, s]), at_z(0))

    def agm_copy(s):
        slot = lax.rem(z + s, 8)
        return remote(fbuf.at[slot], fbuf.at[slot], (agm_sem.at[0, s], agm_sem.at[1, s]), at_z(6))

    agp_copy(0).start()
    agm_copy(0).start()

    eye = iota((128, 128), 0) == iota((128, 128), 1)
    lane = iota((1, 128), 1)

    def column(row):
        return jnp.sum(jnp.where(eye, jnp.broadcast_to(row, (128, 128)), 0.0), axis=1, keepdims=True)

    gate_row = jax.nn.sigmoid(ints[1][0:1].astype(F32) / 64.0)
    gates[...] = jnp.broadcast_to(column(gate_row), (128, 128))
    owner = lax.shift_right_logical(ints[0][0:1], 7) + jnp.where(lane >= 64, 32, 0)
    place = (lax.shift_right_logical(owner, 4) * 2 + (owner & 1)) * 48 + (lax.shift_right_logical(owner, 1) & 7)
    owner_row = owner.astype(F32)
    owner_col = column(owner_row)
    same = jnp.broadcast_to(owner_col, (128, 128)) == jnp.broadcast_to(owner_row, (128, 128))
    before = iota((128, 128), 0) < iota((128, 128), 1)
    after = iota((128, 128), 1) < iota((128, 128), 0)
    rank_row = jnp.sum(jnp.where(same & before, 1.0, 0.0), axis=0, keepdims=True)
    rank_col = jnp.sum(jnp.where(same & after, 1.0, 0.0), axis=1, keepdims=True)
    base_row = place + rank_row.astype(I32) * 8
    base_col = column(place.astype(F32)).astype(I32) + rank_col.astype(I32) * 8
    for t in range(2):
        hit = iota((128, 384), 1) == jnp.broadcast_to(base_col + 24 * t, (128, 384))
        chose[t * 128 : (t + 1) * 128, :] = jnp.where(hit, 1.0, 0.0).astype(BF)
        hit = iota((384, 128), 0) == jnp.broadcast_to(base_row + 24 * t, (384, 128))
        chose_t[:, t * 128 : (t + 1) * 128] = jnp.where(hit, 1.0, 0.0).astype(BF)
    for o in range(8):
        s = iota((48, 384), 0)
        hit = iota((48, 384), 1) == (s & 7) * 48 + (s - (s & 7)) + o
        perm[o * 48 : (o + 1) * 48, :] = jnp.where(hit, 1.0, 0.0).astype(BF)

    each(7, lambda d: selx_copy(d).wait())
    tile = jnp.zeros((8, 128), I32)
    for o in range(8):
        tile = jnp.where(iota((8, 128), 0) == o, selx[o], tile)
    sely[y] = tile

    def sely_copy(d):
        return remote(sely.at[y], sely.at[y], (sely_sem.at[0, d], sely_sem.at[1, d]), at_y(d))

    each(7, lambda d: sely_copy(d).start())
    each(7, lambda d: sely_copy(d).wait())

    block, own = me // 32, lax.rem(me, 32)
    local = sely[...].reshape(64, 128) - own * 128
    wide = iota((64, 128), 1)
    valid = (local >= 0) & (local < 128) & (lax.shift_right_logical(wide, 6) == block)
    lane_f = wide.astype(F32)
    first = jnp.min(jnp.where(valid, lane_f, 999.0), axis=1, keepdims=True)
    rank = lane_f - first
    wanted = [
        jnp.sum(jnp.where(valid & (rank == float(r)), local.astype(F32) + 1000.0, 0.0), axis=1, keepdims=True) - 1000.0
        for r in range(3)
    ]
    rows = []
    for o in range(8):
        for t in range(2):
            for r in range(3):
                want = jnp.broadcast_to(wanted[r][o * 8 : (o + 1) * 8] + 128.0 * t, (8, 256))
                rows.append(jnp.where(iota((8, 256), 1).astype(F32) == want, 1.0, 0.0))
    picked = jnp.concatenate(rows, axis=0)
    pick[...] = picked.astype(BF)
    pick_t[...] = picked.T.astype(BF)

    def y_copy(k, d):
        o = lax.rem(y + d + 1, 8)
        return remote(send1.at[k, o], recv1.at[k, y], (y_sem.at[0, k, d], y_sem.at[1, k, d]), at_y(d))

    def x_copy(k, d):
        o = lax.rem(g + d + 1, 8)
        return remote(send2.at[k, o], recv2.at[k, g], (x_sem.at[0, k, d], x_sem.at[1, k, d]), at_g(d))

    def send_y(k):
        cols = pl.ds(pl.multiple_of(k * 512, 512), 512)
        both = jnp.concatenate([tok[:, cols], cot[:, cols]], axis=0)
        send1[k] = dot(pick[...], both).astype(BF).reshape(8, 48, 512)
        each(7, lambda d: y_copy(k, d).start())
        recv1[k, y] = send1[k, y]

    def multiply(a):
        wide_rows = [
            jnp.concatenate([xs[t, 2 * a], xs[t, 2 * a + 1]], axis=1) for t in range(2)
        ]
        for m in range(3):
            ybuf[m, a] = dot(wide_rows[m // 2], fbuf[:, m].reshape(1024, 512))

    each(AHEAD, send_y)

    def forward(k):
        @pl.when(k < FWD)
        def _():
            each(7, lambda d: y_copy(k, d).wait_recv())
            send2[k] = dot(perm[...], recv1[k].reshape(384, 512)).astype(BF).reshape(8, 48, 512)
            each(7, lambda d: x_copy(k, d).start())
            recv2[k, g] = send2[k, g]

        @pl.when(k + AHEAD < FWD)
        def _():
            send_y(k + AHEAD)

        @pl.when(k < 4)
        def _():
            agp_copy(k).wait_recv()

            @pl.when(k < 3)
            def _():
                agp_copy(k + 1).start()
                agm_copy(k).wait_recv()

            @pl.when(k < 2)
            def _():
                agm_copy(k + 1).start()

        @pl.when(k > 0)
        def _():
            each(7, lambda d: x_copy(k - 1, d).wait_recv())
            both = dot(chose[...], recv2[k - 1].reshape(384, 512)).astype(BF)
            xs[0, k - 1] = both[:128]
            xs[1, k - 1] = both[128:]

        @pl.when(k == 4)
        def _():
            multiply(0)

        @pl.when((k >= 4) & (lax.rem(k, 2) == 0))
        def _():
            multiply(k // 2 - 1)

    each(FWD + 1, forward)

    def middle(block_of_rows):
        at = pl.ds(pl.multiple_of(block_of_rows * 32, 32), 32)

        def combine(m):
            outs = [None] * 4
            for a in range(4):
                for i in range(4):
                    v = ybuf[m, a, at, i * 128 : (i + 1) * 128]
                    for b in range(4):
                        term = mix[0, m, i, a, b] * v
                        outs[b] = term if outs[b] is None else outs[b] + term
            return outs

        gate = gates[at, :]
        pre_gate, pre_up, pulled = combine(0), combine(1), combine(2)
        inner = jnp.zeros((32, 128), F32)
        for b in range(4):
            s = jax.nn.sigmoid(pre_gate[b])
            act = pre_gate[b] * s
            slope = s + act * (1.0 - s)
            hidden = act * pre_up[b]
            inner = inner + hidden * pulled[b]
            back = gate * pulled[b]
            ends[0, b, at, :] = back * pre_up[b] * slope
            ends[1, b, at, :] = back * act
            ends[2, b, at, :] = gate * hidden
        ggs[at, :] = inner
        for m in range(3):
            parts = [ends[m, b, at, :] for b in range(4)]
            for a in range(4):
                for i in range(4):
                    total = mix[0, m, i, a, 0] * parts[0]
                    for b in range(1, 4):
                        total = total + mix[0, m, i, a, b] * parts[b]
                    ubuf[m, a, at, i * 128 : (i + 1) * 128] = total.astype(BF)

    each(4, middle)

    def bx_copy(k, d):
        o = lax.rem(g + d + 1, 8)
        return remote(send3.at[k, o], recv3.at[k, g], (bx_sem.at[0, k, d], bx_sem.at[1, k, d]), at_g(d))

    def by_copy(k, d):
        o = lax.rem(y + d + 1, 8)
        return remote(send4.at[k, o], recv4.at[k, y], (by_sem.at[0, k, d], by_sem.at[1, k, d]), at_y(d))

    def send_bx(a):
        both = jnp.concatenate(
            [
                dot_nt(ubuf[0, a], fbuf[4 * h : 4 * h + 4, 0].reshape(512, 512))
                + dot_nt(ubuf[1, a], fbuf[4 * h : 4 * h + 4, 1].reshape(512, 512))
                for h in range(2)
            ],
            axis=0,
        ).astype(BF)
        send3[a] = dot(chose_t[...], both).astype(BF).reshape(8, 48, 512)
        each(7, lambda d: bx_copy(a, d).start())
        recv3[a, g] = send3[a, g]

    def part(shard, m):
        half = shard // 4
        at = pl.ds(pl.multiple_of(lax.rem(shard, 4) * 128, 128), 128)
        left = jnp.concatenate([xs[m // 2, 2 * a + half, :, at] for a in range(4)], axis=0)
        return dot_tn(left, ubuf[m].reshape(512, 512))

    def rsp_copy(s):
        return remote(plus_s.at[s], plus_r.at[s], (rsp_sem.at[0, s], rsp_sem.at[1, s]), at_z(0))

    def rsm_copy(s):
        return remote(minus_s.at[s], minus_r.at[s], (rsm_sem.at[0, s], rsm_sem.at[1, s]), at_z(6))

    send_bx(0)
    for m in range(3):
        plus_s[0, m] = part(lax.rem(z + 4, 8), m).astype(BF)
    rsp_copy(0).start()
    for m in range(3):
        minus_s[0, m] = part(lax.rem(z + 5, 8), m).astype(BF)
    rsm_copy(0).start()
    each(RET - 1, lambda k: send_bx(k + 1))

    def back(k):
        each(7, lambda d: bx_copy(k, d).wait_recv())
        send4[k] = dot(perm[...], recv3[k].reshape(384, 512)).astype(BF).reshape(8, 48, 512)
        each(7, lambda d: by_copy(k, d).start())
        recv4[k, y] = send4[k, y]

    each(2, back)

    def dots(n):
        m, a = n // 4, lax.rem(n, 4)
        sums = []
        for i in range(4):
            v = ybuf[m, a, :, i * 128 : (i + 1) * 128]
            for b in range(4):
                sums.append(jnp.sum(v * ends[m, b], axis=0, keepdims=True))
        mdrow[pl.ds(pl.multiple_of(n * 16, 16), 16), :] = jnp.concatenate(sums, axis=0)

    mdrow[192:256, :] = jnp.zeros((64, 128), F32)
    each(12, dots)
    mixbuf[z] = lax.dot_general(
        jnp.ones((8, 128), F32), mdrow[...], (((1,), (1,)), ((), ())),
        preferred_element_type=F32, precision=lax.Precision.HIGHEST,
    )

    def mix_copy(d):
        return remote(mixbuf.at[z], mixbuf.at[z], (mix_sem.at[0, d], mix_sem.at[1, d]), at_z(d))

    each(7, lambda d: mix_copy(d).start())

    gate_col = gates[...]
    total_col = jnp.sum(ggs[...], axis=1, keepdims=True) * gate_col * (1.0 - gate_col)
    gate_out[...] = jnp.broadcast_to(jnp.sum(jnp.where(eye, total_col, 0.0), axis=0, keepdims=True), (8, 128))

    def reduce_step(s):
        rsp_copy(s).wait_recv()
        for m in range(3):
            plus_s[s + 1, m] = (part(lax.rem(z + 3 - s, 8), m) + plus_r[s, m].astype(F32)).astype(BF)
        rsp_copy(s + 1).start()

        @pl.when(s < 2)
        def _():
            rsm_copy(s).wait_recv()
            for m in range(3):
                minus_s[s + 1, m] = (part(lax.rem(z + 6 + s, 8), m) + minus_r[s, m].astype(F32)).astype(BF)
            rsm_copy(s + 1).start()

    def arrive(k):
        each(7, lambda d: by_copy(k, d).wait_recv())
        both = dot(pick_t[...], recv4[k].reshape(384, 512)).astype(BF)
        for h in range(2):
            tok_out[:, pl.ds(pl.multiple_of(k * 1024 + h * 512, 512), 512)] = both[h * 128 : (h + 1) * 128]

    reduce_step(0)
    back(2)
    back(3)
    each(2, lambda s: (arrive(s), reduce_step(s + 1)))
    each(2, lambda s: arrive(s + 2))
    rsp_copy(3).wait_recv()
    rsm_copy(2).wait_recv()
    for m in range(3):
        total = part(z, m) + plus_r[3, m].astype(F32) + minus_r[2, m].astype(F32)
        for i in range(4):
            fac_out[0, m, i] = total[:, i * 128 : (i + 1) * 128]

    each(7, lambda d: mix_copy(d).wait_recv())
    total = mixbuf[0]
    for o in range(1, 8):
        total = total + mixbuf[o]
    mix_out[...] = total

    each(7, lambda d: mix_copy(d).wait_send())
    each(FWD, lambda k: each(7, lambda d: (y_copy(k, d).wait_send(), x_copy(k, d).wait_send())))
    each(RET, lambda k: each(7, lambda d: (bx_copy(k, d).wait_send(), by_copy(k, d).wait_send())))
    each(4, lambda s: (agp_copy(s).wait_send(), rsp_copy(s).wait_send()))
    each(3, lambda s: (agm_copy(s).wait_send(), rsm_copy(s).wait_send()))


def shards(tokens, cotangent, factors, mix, selection, scores):
    ints = jnp.broadcast_to(
        jnp.concatenate([selection.reshape(1, 1, 128), scores.reshape(1, 1, 128)], axis=0), (2, 8, 128)
    )
    vmem = pl.BlockSpec(memory_space=pltpu.VMEM)
    dma = pltpu.SemaphoreType.DMA
    row = (8, 48, 512)
    token_grad, factor_grad, mixed, gated = pl.pallas_call(
        kernel,
        out_shape=(
            jax.ShapeDtypeStruct((128, 4096), BF),
            jax.ShapeDtypeStruct((1, 3, 4, 128, 128), F32),
            jax.ShapeDtypeStruct((8, 256), F32),
            jax.ShapeDtypeStruct((8, 128), F32),
        ),
        in_specs=[vmem, vmem, vmem, pl.BlockSpec(memory_space=pltpu.SMEM), vmem],
        out_specs=(vmem, vmem, vmem, vmem),
        scratch_shapes=[
            pltpu.VMEM((8, 8, 128), I32),
            pltpu.VMEM((8, 8, 128), I32),
            pltpu.VMEM((384, 256), BF),
            pltpu.VMEM((256, 384), BF),
            pltpu.VMEM((256, 384), BF),
            pltpu.VMEM((384, 256), BF),
            pltpu.VMEM((384, 384), BF),
            *[pltpu.VMEM((FWD,) + row, BF)] * 4,
            *[pltpu.VMEM((RET,) + row, BF)] * 4,
            pltpu.VMEM((8, 3, 128, 512), BF),
            pltpu.VMEM((2, FWD, 128, 512), BF),
            pltpu.VMEM((3, 4, 128, 512), F32),
            pltpu.VMEM((3, 4, 128, 512), BF),
            pltpu.VMEM((3, 4, 128, 128), F32),
            pltpu.VMEM((128, 128), F32),
            pltpu.VMEM((128, 128), F32),
            pltpu.VMEM((256, 128), F32),
            pltpu.VMEM((8, 8, 256), F32),
            *[pltpu.VMEM((4, 3, 128, 512), BF)] * 2,
            *[pltpu.VMEM((3, 3, 128, 512), BF)] * 2,
            dma((2, 7)),
            dma((2, 7)),
            dma((2, FWD, 7)),
            dma((2, FWD, 7)),
            dma((2, RET, 7)),
            dma((2, RET, 7)),
            dma((2, 4)),
            dma((2, 3)),
            dma((2, 4)),
            dma((2, 3)),
            dma((2, 7)),
        ],
        compiler_params=pltpu.CompilerParams(
            collective_id=0, has_side_effects=True, vmem_limit_bytes=58 << 20
        ),
    )(tokens, cotangent, factors, mix, ints)
    mix_grad = mixed[0, :192].reshape(1, 3, 4, 4, 4).transpose(0, 1, 3, 2, 4)
    return token_grad, factor_grad, mix_grad, gated[0].reshape(1, 2, 64)


def solution(mesh):
    return jax.shard_map(
        shards,
        mesh=mesh,
        in_specs=(
            P(("seq", "exp"), None),
            P(("seq", "exp"), None),
            P("exp", None, None, "seq", None),
            P("exp", None, None, None, None),
            P("exp", "seq", None),
            P("exp", "seq", None),
        ),
        out_specs=(
            P(("seq", "exp"), None),
            P("exp", None, None, "seq", None),
            P("exp", None, None, None, None),
            P("exp", "seq", None),
        ),
        check_vma=False,
    )
```

```python
import jax
import jax.numpy as jnp
from jax import lax
from jax.experimental import pallas as pl
from jax.experimental.pallas import tpu as pltpu
from jax.sharding import PartitionSpec as P

MESH = pl.DeviceIdType.MESH
BF = jnp.bfloat16
F32 = jnp.float32
I32 = jnp.int32
FWD = 8
RET = 4
LATE = 6
AHEAD = 3


def dot(a, b):
    return lax.dot_general(a, b, (((1,), (0,)), ((), ())), preferred_element_type=F32)


def dot_nt(a, b):
    return lax.dot_general(a, b, (((1,), (1,)), ((), ())), preferred_element_type=F32)


def dot_tn(a, b):
    return lax.dot_general(a, b, (((0,), (0,)), ((), ())), preferred_element_type=F32)


def iota(shape, dim):
    return lax.broadcasted_iota(I32, shape, dim)


def each(n, body):
    lax.fori_loop(0, n, lambda d, carry: (body(d), carry)[1], 0)


def kernel(
    tok_in, cot_in, fac_in, mix_in, sel_in, sco_in, tok_out, fac_out, mix_out, gate_out,
    tok, cot, fac, mix, selection, scores, selx, sely, pick, pick_t, chose, chose_t, perm, pick2, pick2_t, chose2, chose2_t,
    send1, recv1, send2, recv2, send3, recv3, send4, recv4,
    fbuf, xs, ybuf, ubuf, ends, gates, ggs, mdrow, mixbuf,
    plus_s, plus_r, minus_s, minus_r,
    in_sem, selx_sem, sely_sem, y_sem, x_sem, bx_sem, by_sem, agp_sem, agm_sem, rsp_sem, rsm_sem, mix_sem,
):
    loads = [
        pltpu.make_async_copy(src, dst, in_sem.at[n])
        for n, (src, dst) in enumerate(
            ((sel_in, selection), (fac_in, fac), (tok_in, tok), (cot_in, cot), (sco_in, scores), (mix_in, mix))
        )
    ]
    for load in loads:
        load.start()
    me = lax.axis_index("exp")
    z = lax.axis_index("seq")
    core, y, x = lax.rem(me, 2), lax.rem(me // 2, 8), me // 16
    g = x * 2 + core

    def at_y(d):
        return {"exp": (x * 8 + lax.rem(y + d + 1, 8)) * 2 + core, "seq": z}

    def at_g(d):
        o = lax.rem(g + d + 1, 8)
        return {"exp": ((o // 2) * 8 + y) * 2 + lax.rem(o, 2), "seq": z}

    def at_z(d):
        return {"exp": me, "seq": lax.rem(z + d + 1, 8)}

    def remote(src, dst, sems, where):
        return pltpu.make_async_remote_copy(
            src_ref=src, dst_ref=dst, send_sem=sems[0], recv_sem=sems[1],
            device_id=where, device_id_type=MESH,
        )

    barrier = pltpu.get_barrier_semaphore()
    for place in (at_g, at_y, at_z):
        each(7, lambda d, place=place: pl.semaphore_signal(barrier, inc=1, device_id=place(d), device_id_type=MESH))
    for o in range(8):
        s = iota((48, 384), 0)
        hit = iota((48, 384), 1) == (s & 7) * 48 + (s - (s & 7)) + o
        perm[o * 48 : (o + 1) * 48, :] = jnp.where(hit, 1.0, 0.0).astype(BF)
    pl.semaphore_wait(barrier, 21)

    def selx_copy(d):
        return remote(selx.at[g], selx.at[g], (selx_sem.at[0, d], selx_sem.at[1, d]), at_g(d))

    def joined(ref):
        return jnp.concatenate([ref[0, 0:1], ref[0, 1:2]], axis=1)

    loads[0].wait()
    chosen = joined(selection)
    selx[g] = jnp.broadcast_to(chosen, (8, 128))
    each(7, lambda d: selx_copy(d).start())

    loads[1].wait()
    for m in range(3):
        for i in range(4):
            fbuf[z, m, :, i * 128 : (i + 1) * 128] = fac[0, m, i]

    def agp_copy(s):
        slot = lax.rem(z - s + 8, 8)
        return remote(fbuf.at[slot], fbuf.at[slot], (agp_sem.at[0, s], agp_sem.at[1, s]), at_z(0))

    def agm_copy(s):
        slot = lax.rem(z + s, 8)
        return remote(fbuf.at[slot], fbuf.at[slot], (agm_sem.at[0, s], agm_sem.at[1, s]), at_z(6))

    agp_copy(0).start()
    agm_copy(0).start()

    each(7, lambda d: selx_copy(d).wait())
    tile = jnp.zeros((8, 128), I32)
    for o in range(8):
        tile = jnp.where(iota((8, 128), 0) == o, selx[o], tile)
    sely[y] = tile

    def sely_copy(d):
        return remote(sely.at[y], sely.at[y], (sely_sem.at[0, d], sely_sem.at[1, d]), at_y(d))

    each(7, lambda d: sely_copy(d).start())
    eye = iota((128, 128), 0) == iota((128, 128), 1)
    lane = iota((1, 128), 1)

    def column(row):
        return jnp.sum(jnp.where(eye, jnp.broadcast_to(row, (128, 128)), 0.0), axis=1, keepdims=True)

    loads[4].wait()
    gate_row = jax.nn.sigmoid(joined(scores).astype(F32) / 64.0)
    gates[...] = jnp.broadcast_to(column(gate_row), (128, 128))
    owner = lax.shift_right_logical(chosen, 7) + jnp.where(lane >= 64, 32, 0)
    place = (lax.shift_right_logical(owner, 4) * 2 + (owner & 1)) * 48 + (lax.shift_right_logical(owner, 1) & 7)
    owner_row = owner.astype(F32)
    owner_col = column(owner_row)
    same = jnp.broadcast_to(owner_col, (128, 128)) == jnp.broadcast_to(owner_row, (128, 128))
    before = iota((128, 128), 0) < iota((128, 128), 1)
    after = iota((128, 128), 1) < iota((128, 128), 0)
    rank_row = jnp.sum(jnp.where(same & before, 1.0, 0.0), axis=0, keepdims=True)
    rank_col = jnp.sum(jnp.where(same & after, 1.0, 0.0), axis=1, keepdims=True)
    base_row = place + rank_row.astype(I32) * 8
    base_col = column(place.astype(F32)).astype(I32) + rank_col.astype(I32) * 8
    each(7, lambda d: sely_copy(d).wait())

    block, own = me // 32, lax.rem(me, 32)
    local = sely[...].reshape(64, 128) - own * 128
    wide = iota((64, 128), 1)
    valid = (local >= 0) & (local < 128) & (lax.shift_right_logical(wide, 6) == block)
    lane_f = wide.astype(F32)
    first = jnp.min(jnp.where(valid, lane_f, 999.0), axis=1, keepdims=True)
    rank = lane_f - first
    wanted = [
        jnp.sum(jnp.where(valid & (rank == float(r)), local.astype(F32) + 1000.0, 0.0), axis=1, keepdims=True) - 1000.0
        for r in range(3)
    ]
    rows = []
    for o in range(8):
        for t in range(2):
            for r in range(3):
                want = jnp.broadcast_to(wanted[r][o * 8 : (o + 1) * 8] + 128.0 * t, (8, 256))
                rows.append(jnp.where(iota((8, 256), 1).astype(F32) == want, 1.0, 0.0))
    picked = jnp.concatenate(rows, axis=0)
    pick[...] = picked.astype(BF)

    def y_copy(k, d, late):
        o = lax.rem(y + d + 1, 8)
        src, dst = (send2, recv2) if late else (send1, recv1)
        return remote(src.at[k, o], dst.at[k, y], (y_sem.at[0, k, d], y_sem.at[1, k, d]), at_y(d))

    def x_copy(k, d, late):
        o = lax.rem(g + d + 1, 8)
        src, dst = (send1, recv1) if late else (send2, recv2)
        return remote(src.at[k, o], dst.at[k, g], (x_sem.at[0, k, d], x_sem.at[1, k, d]), at_g(d))

    def first(k, late):
        cols = pl.ds(pl.multiple_of(k * 512, 512), 512)
        both = jnp.concatenate([tok[:, cols], cot[:, cols]], axis=0)
        send1[k] = dot((pick2 if late else pick)[...], both).astype(BF).reshape(8, 48, 512)
        copy, own = (x_copy, g) if late else (y_copy, y)
        each(7, lambda d: copy(k, d, late).start())
        recv1[k, own] = send1[k, own]

    def second(k, late):
        copy, then, own = (x_copy, y_copy, y) if late else (y_copy, x_copy, g)
        each(7, lambda d: copy(k, d, late).wait_recv())
        send2[k] = dot(perm[...], recv1[k].reshape(384, 512)).astype(BF).reshape(8, 48, 512)
        each(7, lambda d: then(k, d, late).start())
        recv2[k, own] = send2[k, own]

    def land(k, late):
        copy = y_copy if late else x_copy
        each(7, lambda d: copy(k, d, late).wait_recv())
        both = dot((chose2 if late else chose)[...], recv2[k].reshape(384, 512)).astype(BF)
        xs[0, k] = both[:128]
        xs[1, k] = both[128:]

    def multiply(k):
        a, h = k // 2, lax.rem(k, 2)
        for m in range(3):
            out = dot(xs[m // 2, k], fbuf[pl.ds(h * 4, 4), m].reshape(512, 512))

            @pl.when(h == 0)
            def _():
                ybuf[m, a] = out

            @pl.when(h == 1)
            def _():
                ybuf[m, a] += out

    loads[2].wait()
    loads[3].wait()
    first(0, False)
    first(1, False)
    pick2[...] = dot(perm[...], pick[...]).astype(BF)
    each(FWD - LATE, lambda k: first(k + LATE, True))
    first(2, False)
    for t in range(2):
        hit = iota((128, 384), 1) == jnp.broadcast_to(base_col + 24 * t, (128, 384))
        chose[t * 128 : (t + 1) * 128, :] = jnp.where(hit, 1.0, 0.0).astype(BF)
        hit = iota((384, 128), 0) == jnp.broadcast_to(base_row + 24 * t, (384, 128))
        chose_t[:, t * 128 : (t + 1) * 128] = jnp.where(hit, 1.0, 0.0).astype(BF)
    chose2[...] = dot(chose[...], perm[...]).astype(BF)
    chose2_t[...] = dot(perm[...], chose_t[...]).astype(BF)
    pick_t[...] = picked.T.astype(BF)
    pick2_t[...] = dot(pick_t[...], perm[...]).astype(BF)

    def forward(k):
        second(k, False)

        @pl.when(k + AHEAD < LATE)
        def _():
            first(k + AHEAD, False)

        @pl.when((k + AHEAD >= LATE) & (k + AHEAD < FWD))
        def _():
            second(k + AHEAD, True)

        @pl.when(k < 4)
        def _():
            agp_copy(k).wait_recv()

            @pl.when(k < 3)
            def _():
                agp_copy(k + 1).start()
                agm_copy(k).wait_recv()

            @pl.when(k < 2)
            def _():
                agm_copy(k + 1).start()

        @pl.when(k > 0)
        def _():
            land(k - 1, False)

        @pl.when(k == 4)
        def _():
            each(4, multiply)

        @pl.when(k == 5)
        def _():
            multiply(k - 1)

    each(LATE, forward)
    land(LATE - 1, False)
    multiply(LATE - 1)

    def finish(k):
        land(k + LATE, True)
        multiply(k + LATE)

    each(FWD - LATE, finish)

    loads[5].wait()

    def middle(block_of_rows):
        at = pl.ds(pl.multiple_of(block_of_rows * 32, 32), 32)

        def combine(m):
            outs = [None] * 4
            for a in range(4):
                for i in range(4):
                    v = ybuf[m, a, at, i * 128 : (i + 1) * 128]
                    for b in range(4):
                        term = mix[0, m, i, a, b] * v
                        outs[b] = term if outs[b] is None else outs[b] + term
            return outs

        gate = gates[at, :]
        pre_gate, pre_up, pulled = combine(0), combine(1), combine(2)
        inner = jnp.zeros((32, 128), F32)
        for b in range(4):
            s = jax.nn.sigmoid(pre_gate[b])
            act = pre_gate[b] * s
            slope = s + act * (1.0 - s)
            hidden = act * pre_up[b]
            inner = inner + hidden * pulled[b]
            back = gate * pulled[b]
            ends[0, b, at, :] = back * pre_up[b] * slope
            ends[1, b, at, :] = back * act
            ends[2, b, at, :] = gate * hidden
        ggs[at, :] = inner
        for m in range(3):
            parts = [ends[m, b, at, :] for b in range(4)]
            for a in range(4):
                for i in range(4):
                    total = mix[0, m, i, a, 0] * parts[0]
                    for b in range(1, 4):
                        total = total + mix[0, m, i, a, b] * parts[b]
                    ubuf[m, a, at, i * 128 : (i + 1) * 128] = total.astype(BF)

    each(4, middle)

    def bx_copy(k, d, early):
        o = lax.rem(g + d + 1, 8)
        src, dst = (send4, recv4) if early else (send3, recv3)
        return remote(src.at[k, o], dst.at[k, g], (bx_sem.at[0, k, d], bx_sem.at[1, k, d]), at_g(d))

    def by_copy(k, d, early):
        o = lax.rem(y + d + 1, 8)
        src, dst = (send3, recv3) if early else (send4, recv4)
        return remote(src.at[k, o], dst.at[k, y], (by_sem.at[0, k, d], by_sem.at[1, k, d]), at_y(d))

    def leave(a, early):
        both = jnp.concatenate(
            [
                dot_nt(ubuf[0, a], fbuf[4 * h : 4 * h + 4, 0].reshape(512, 512))
                + dot_nt(ubuf[1, a], fbuf[4 * h : 4 * h + 4, 1].reshape(512, 512))
                for h in range(2)
            ],
            axis=0,
        ).astype(BF)
        send3[a] = dot((chose2_t if early else chose_t)[...], both).astype(BF).reshape(8, 48, 512)
        copy, own = (by_copy, y) if early else (bx_copy, g)
        each(7, lambda d: copy(a, d, early).start())
        recv3[a, own] = send3[a, own]

    def turn(k, early):
        copy, then, own = (by_copy, bx_copy, g) if early else (bx_copy, by_copy, y)
        each(7, lambda d: copy(k, d, early).wait_recv())
        send4[k] = dot(perm[...], recv3[k].reshape(384, 512)).astype(BF).reshape(8, 48, 512)
        each(7, lambda d: then(k, d, early).start())
        recv4[k, own] = send4[k, own]

    def arrive(k, early):
        copy = bx_copy if early else by_copy
        each(7, lambda d: copy(k, d, early).wait_recv())
        both = dot((pick2_t if early else pick_t)[...], recv4[k].reshape(384, 512)).astype(BF)
        for h in range(2):
            tok_out[:, k * 1024 + h * 512 : k * 1024 + h * 512 + 512] = both[h * 128 : (h + 1) * 128]

    def part(shard, m):
        half = shard // 4
        at = pl.ds(pl.multiple_of(lax.rem(shard, 4) * 128, 128), 128)
        left = jnp.concatenate([xs[m // 2, 2 * a + half, :, at] for a in range(4)], axis=0)
        return dot_tn(left, ubuf[m].reshape(512, 512))

    def rs_copy(way, s, m):
        src, dst, sems = ((plus_s, plus_r, rsp_sem), (minus_s, minus_r, rsm_sem))[way]
        at = pl.ds(64 * way, 64) if s == 0 else pl.ds(0, 128)
        return remote(src.at[s, m, at], dst.at[s, m, at], (sems.at[0, s, m], sems.at[1, s, m]), at_z(6 * way))

    def reduce_first(m):
        far = part(lax.rem(z + 4, 8), m)
        for way, src in ((0, plus_s), (1, minus_s)):
            src[0, m, 64 * way : 64 * way + 64] = far[64 * way : 64 * way + 64].astype(BF)
            rs_copy(way, 0, m).start()

    def reduce_next(s, m):
        for way, src, got in ((0, plus_s, plus_r), (1, minus_s, minus_r)):
            own = part(lax.rem(z + 4 + (s if way else 8 - s), 8), m)
            rs_copy(way, s - 1, m).wait_recv()
            if s == 1:
                near = own[64 * way : 64 * way + 64] + got[0, m, 64 * way : 64 * way + 64].astype(F32)
                src[1, m, 64 * way : 64 * way + 64] = near.astype(BF)
                src[1, m, 64 - 64 * way : 128 - 64 * way] = own[64 - 64 * way : 128 - 64 * way].astype(BF)
            else:
                src[s, m] = (own + got[s - 1, m].astype(F32)).astype(BF)
            rs_copy(way, s, m).start()

    def reduce_last(m):
        total = part(z, m)
        rs_copy(0, 3, m).wait_recv()
        rs_copy(1, 3, m).wait_recv()
        total = total + plus_r[3, m].astype(F32) + minus_r[3, m].astype(F32)
        for i in range(4):
            fac_out[0, m, i] = total[:, i * 128 : (i + 1) * 128]

    def dots(n):
        m, a = n // 4, lax.rem(n, 4)
        for i in range(4):
            v = ybuf[m, a, :, i * 128 : (i + 1) * 128]
            for b in range(4):
                mdrow[b, pl.ds(m * 16 + i * 4 + a, 1), :] = jnp.sum(v * ends[m, b], axis=0, keepdims=True)

    def mix_copy(d):
        return remote(mixbuf.at[z], mixbuf.at[z], (mix_sem.at[0, d], mix_sem.at[1, d]), at_z(d))

    leave(0, True)
    leave(1, False)
    for m in range(3):
        reduce_first(m)
    leave(2, False)
    reduce_next(1, 0)
    turn(1, False)
    reduce_next(1, 1)
    reduce_next(1, 2)
    leave(3, False)
    reduce_next(2, 0)
    turn(0, True)
    turn(2, False)
    reduce_next(2, 1)
    reduce_next(2, 2)
    turn(3, False)
    arrive(0, True)
    reduce_next(3, 0)
    arrive(1, False)
    reduce_next(3, 1)
    reduce_next(3, 2)

    each(12, dots)
    small = jnp.zeros((48, 128), F32)
    for b in range(4):
        small = jnp.where(iota((48, 128), 1) == b, jnp.sum(mdrow[b], axis=1, keepdims=True), small)
    mixbuf[z] = small
    each(7, lambda d: mix_copy(d).start())
    gate_col = gates[...]
    total_col = jnp.sum(ggs[...], axis=1, keepdims=True) * gate_col * (1.0 - gate_col)
    total_row = jnp.sum(jnp.where(eye, total_col, 0.0), axis=0, keepdims=True)
    gate_out[0, 0:1] = total_row[:, :64]
    gate_out[0, 1:2] = total_row[:, 64:]

    reduce_last(0)
    arrive(2, False)
    reduce_last(1)
    reduce_last(2)
    each(7, lambda d: mix_copy(d).wait_recv())
    total = mixbuf[0]
    for o in range(1, 8):
        total = total + mixbuf[o]
    for m in range(3):
        for i in range(4):
            at = (m * 4 + i) * 4
            mix_out[0, m, i] = total[at : at + 4, :4]
    arrive(3, False)

    each(7, lambda d: mix_copy(d).wait_send())
    each(LATE, lambda k: each(7, lambda d: (y_copy(k, d, False).wait_send(), x_copy(k, d, False).wait_send())))
    each(FWD - LATE, lambda k: each(7, lambda d: (y_copy(k + LATE, d, True).wait_send(), x_copy(k + LATE, d, True).wait_send())))
    each(7, lambda d: (bx_copy(0, d, True).wait_send(), by_copy(0, d, True).wait_send()))
    each(RET - 1, lambda k: each(7, lambda d: (bx_copy(k + 1, d, False).wait_send(), by_copy(k + 1, d, False).wait_send())))
    each(4, lambda s: agp_copy(s).wait_send())
    each(3, lambda s: agm_copy(s).wait_send())
    for s in range(4):
        each(3, lambda m, s=s: (rs_copy(0, s, m).wait_send(), rs_copy(1, s, m).wait_send()))


def shards(tokens, cotangent, factors, mix, selection, scores):
    vmem = pl.BlockSpec(memory_space=pltpu.VMEM)
    hbm = pl.BlockSpec(memory_space=pltpu.HBM)
    dma = pltpu.SemaphoreType.DMA
    row = (8, 48, 512)
    return pl.pallas_call(
        kernel,
        out_shape=(
            jax.ShapeDtypeStruct((128, 4096), BF),
            jax.ShapeDtypeStruct((1, 3, 4, 128, 128), F32),
            jax.ShapeDtypeStruct((1, 3, 4, 4, 4), F32),
            jax.ShapeDtypeStruct((1, 2, 64), F32),
        ),
        in_specs=[hbm] * 6,
        out_specs=(vmem, vmem, vmem, vmem),
        scratch_shapes=[
            *[pltpu.VMEM((128, 4096), BF)] * 2,
            pltpu.VMEM((1, 3, 4, 128, 128), BF),
            pltpu.SMEM((1, 3, 4, 4, 4), F32),
            *[pltpu.VMEM((1, 2, 64), I32)] * 2,
            pltpu.VMEM((8, 8, 128), I32),
            pltpu.VMEM((8, 8, 128), I32),
            pltpu.VMEM((384, 256), BF),
            pltpu.VMEM((256, 384), BF),
            pltpu.VMEM((256, 384), BF),
            pltpu.VMEM((384, 256), BF),
            pltpu.VMEM((384, 384), BF),
            pltpu.VMEM((384, 256), BF),
            pltpu.VMEM((256, 384), BF),
            pltpu.VMEM((256, 384), BF),
            pltpu.VMEM((384, 256), BF),
            *[pltpu.VMEM((FWD,) + row, BF)] * 4,
            *[pltpu.VMEM((RET,) + row, BF)] * 4,
            pltpu.VMEM((8, 3, 128, 512), BF),
            pltpu.VMEM((2, FWD, 128, 512), BF),
            pltpu.VMEM((3, 4, 128, 512), F32),
            pltpu.VMEM((3, 4, 128, 512), BF),
            pltpu.VMEM((3, 4, 128, 128), F32),
            pltpu.VMEM((128, 128), F32),
            pltpu.VMEM((128, 128), F32),
            pltpu.VMEM((4, 48, 128), F32),
            pltpu.VMEM((8, 48, 128), F32),
            *[pltpu.VMEM((4, 3, 128, 512), BF)] * 4,
            dma((6,)),
            dma((2, 7)),
            dma((2, 7)),
            dma((2, FWD, 7)),
            dma((2, FWD, 7)),
            dma((2, RET, 7)),
            dma((2, RET, 7)),
            dma((2, 4)),
            dma((2, 3)),
            dma((2, 4, 3)),
            dma((2, 4, 3)),
            dma((2, 7)),
        ],
        compiler_params=pltpu.CompilerParams(
            collective_id=0, has_side_effects=True, vmem_limit_bytes=46 << 20
        ),
    )(*[pltpu.with_memory_space_constraint(v, pltpu.HBM) for v in (tokens, cotangent, factors, mix, selection, scores)])


def solution(mesh):
    return jax.shard_map(
        shards,
        mesh=mesh,
        in_specs=(
            P(("seq", "exp"), None),
            P(("seq", "exp"), None),
            P("exp", None, None, "seq", None),
            P("exp", None, None, None, None),
            P("exp", "seq", None),
            P("exp", "seq", None),
        ),
        out_specs=(
            P(("seq", "exp"), None),
            P("exp", None, None, "seq", None),
            P("exp", None, None, None, None),
            P("exp", "seq", None),
        ),
        check_vma=False,
    )
```

```python
import jax
import jax.numpy as jnp
from jax import lax
from jax.experimental import pallas as pl
from jax.experimental.pallas import tpu as pltpu
from jax.sharding import PartitionSpec as P

MESH = pl.DeviceIdType.MESH
BF = jnp.bfloat16
F32 = jnp.float32
I32 = jnp.int32
FWD = 8
RET = 4
EARLY = 2
LATE = 6
AHEAD = 3


def dot(a, b):
    return lax.dot_general(a, b, (((1,), (0,)), ((), ())), preferred_element_type=F32)


def dot_nt(a, b):
    return lax.dot_general(a, b, (((1,), (1,)), ((), ())), preferred_element_type=F32)


def dot_tn(a, b):
    return lax.dot_general(a, b, (((0,), (0,)), ((), ())), preferred_element_type=F32)


def iota(shape, dim):
    return lax.broadcasted_iota(I32, shape, dim)


def each(n, body):
    lax.fori_loop(0, n, lambda d, carry: (body(d), carry)[1], 0)


def kernel(
    tok_in, cot_in, fac_in, mix_in, sel_in, sco_in, tok_out, fac_out, mix_out, gate_out,
    tok, cot, fac, mix, selection, scores, selx, sely, pick, pick_t, chose, chose_t, perm, pick2, pick2_t, chose2, chose2_t,
    send1, recv1, send2, recv2, send3, recv3, send4, recv4,
    fbuf, xs, ybuf, ubuf, ends, gates, ggs, mdrow, mixbuf,
    plus_s, plus_r, minus_s, minus_r,
    in_sem, selx_sem, sely_sem, y_sem, x_sem, bx_sem, by_sem, agp_sem, agm_sem, rsp_sem, rsm_sem, mix_sem,
):
    loads = [
        pltpu.make_async_copy(src, dst, in_sem.at[n])
        for n, (src, dst) in enumerate(
            ((sel_in, selection), (fac_in, fac), (tok_in, tok), (cot_in, cot), (sco_in, scores), (mix_in, mix))
        )
    ]
    for load in loads:
        load.start()
    me = lax.axis_index("exp")
    z = lax.axis_index("seq")
    core, y, x = lax.rem(me, 2), lax.rem(me // 2, 8), me // 16
    g = x * 2 + core

    def at_y(d):
        return {"exp": (x * 8 + lax.rem(y + d + 1, 8)) * 2 + core, "seq": z}

    def at_g(d):
        o = lax.rem(g + d + 1, 8)
        return {"exp": ((o // 2) * 8 + y) * 2 + lax.rem(o, 2), "seq": z}

    def at_z(d):
        return {"exp": me, "seq": lax.rem(z + d + 1, 8)}

    def remote(src, dst, sems, where):
        return pltpu.make_async_remote_copy(
            src_ref=src, dst_ref=dst, send_sem=sems[0], recv_sem=sems[1],
            device_id=where, device_id_type=MESH,
        )

    barrier = pltpu.get_barrier_semaphore()
    for place in (at_g, at_y, at_z):
        each(7, lambda d, place=place: pl.semaphore_signal(barrier, inc=1, device_id=place(d), device_id_type=MESH))
    for o in range(8):
        s = iota((48, 384), 0)
        hit = iota((48, 384), 1) == (s & 7) * 48 + (s - (s & 7)) + o
        perm[o * 48 : (o + 1) * 48, :] = jnp.where(hit, 1.0, 0.0).astype(BF)
    pl.semaphore_wait(barrier, 21)

    def selx_copy(d):
        return remote(selx.at[g], selx.at[g], (selx_sem.at[0, d], selx_sem.at[1, d]), at_g(d))

    def joined(ref):
        return jnp.concatenate([ref[0, 0:1], ref[0, 1:2]], axis=1)

    loads[0].wait()
    chosen = joined(selection)
    selx[g] = jnp.broadcast_to(chosen, (8, 128))
    each(7, lambda d: selx_copy(d).start())

    each(7, lambda d: selx_copy(d).wait())
    tile = jnp.zeros((8, 128), I32)
    for o in range(8):
        tile = jnp.where(iota((8, 128), 0) == o, selx[o], tile)
    sely[y] = tile

    def sely_copy(d):
        return remote(sely.at[y], sely.at[y], (sely_sem.at[0, d], sely_sem.at[1, d]), at_y(d))

    each(7, lambda d: sely_copy(d).start())

    loads[1].wait()
    for m in range(3):
        for i in range(4):
            fbuf[z, m, :, i * 128 : (i + 1) * 128] = fac[0, m, i]

    def agp_copy(s):
        slot = lax.rem(z - s + 8, 8)
        return remote(fbuf.at[slot], fbuf.at[slot], (agp_sem.at[0, s], agp_sem.at[1, s]), at_z(0))

    def agm_copy(s):
        slot = lax.rem(z + s, 8)
        return remote(fbuf.at[slot], fbuf.at[slot], (agm_sem.at[0, s], agm_sem.at[1, s]), at_z(6))

    agp_copy(0).start()
    agm_copy(0).start()

    eye = iota((128, 128), 0) == iota((128, 128), 1)
    lane = iota((1, 128), 1)

    def column(row):
        return jnp.sum(jnp.where(eye, jnp.broadcast_to(row, (128, 128)), 0.0), axis=1, keepdims=True)

    loads[4].wait()
    gate_row = jax.nn.sigmoid(joined(scores).astype(F32) / 64.0)
    gates[...] = jnp.broadcast_to(column(gate_row), (128, 128))
    owner = lax.shift_right_logical(chosen, 7) + jnp.where(lane >= 64, 32, 0)
    place = (lax.shift_right_logical(owner, 4) * 2 + (owner & 1)) * 48 + (lax.shift_right_logical(owner, 1) & 7)
    owner_row = owner.astype(F32)
    owner_col = column(owner_row)
    same = jnp.broadcast_to(owner_col, (128, 128)) == jnp.broadcast_to(owner_row, (128, 128))
    before = iota((128, 128), 0) < iota((128, 128), 1)
    after = iota((128, 128), 1) < iota((128, 128), 0)
    rank_row = jnp.sum(jnp.where(same & before, 1.0, 0.0), axis=0, keepdims=True)
    rank_col = jnp.sum(jnp.where(same & after, 1.0, 0.0), axis=1, keepdims=True)
    base_row = place + rank_row.astype(I32) * 8
    base_col = column(place.astype(F32)).astype(I32) + rank_col.astype(I32) * 8
    each(7, lambda d: sely_copy(d).wait())

    block, own = me // 32, lax.rem(me, 32)
    local = sely[...].reshape(64, 128) - own * 128
    wide = iota((64, 128), 1)
    valid = (local >= 0) & (local < 128) & (lax.shift_right_logical(wide, 6) == block)
    lane_f = wide.astype(F32)
    first = jnp.min(jnp.where(valid, lane_f, 999.0), axis=1, keepdims=True)
    rank = lane_f - first
    wanted = [
        jnp.sum(jnp.where(valid & (rank == float(r)), local.astype(F32) + 1000.0, 0.0), axis=1, keepdims=True) - 1000.0
        for r in range(3)
    ]
    rows = []
    for o in range(8):
        for t in range(2):
            for r in range(3):
                want = jnp.broadcast_to(wanted[r][o * 8 : (o + 1) * 8] + 128.0 * t, (8, 256))
                rows.append(jnp.where(iota((8, 256), 1).astype(F32) == want, 1.0, 0.0))
    picked = jnp.concatenate(rows, axis=0)
    pick[...] = picked.astype(BF)

    def y_copy(k, d, late):
        o = lax.rem(y + d + 1, 8)
        src, dst = (send2, recv2) if late else (send1, recv1)
        return remote(src.at[k, o], dst.at[k, y], (y_sem.at[0, k, d], y_sem.at[1, k, d]), at_y(d))

    def x_copy(k, d, late):
        o = lax.rem(g + d + 1, 8)
        src, dst = (send1, recv1) if late else (send2, recv2)
        return remote(src.at[k, o], dst.at[k, g], (x_sem.at[0, k, d], x_sem.at[1, k, d]), at_g(d))

    def first(k, late):
        cols = pl.ds(pl.multiple_of(k * 512, 512), 512)
        both = jnp.concatenate([tok[:, cols], cot[:, cols]], axis=0)
        send1[k] = dot((pick2 if late else pick)[...], both).astype(BF).reshape(8, 48, 512)
        copy, own = (x_copy, g) if late else (y_copy, y)
        each(7, lambda d: copy(k, d, late).start())
        recv1[k, own] = send1[k, own]

    def second(k, late):
        copy, then, own = (x_copy, y_copy, y) if late else (y_copy, x_copy, g)
        each(7, lambda d: copy(k, d, late).wait_recv())
        send2[k] = dot(perm[...], recv1[k].reshape(384, 512)).astype(BF).reshape(8, 48, 512)
        each(7, lambda d: then(k, d, late).start())
        recv2[k, own] = send2[k, own]

    def land(k, late):
        copy = y_copy if late else x_copy
        each(7, lambda d: copy(k, d, late).wait_recv())
        both = dot((chose2 if late else chose)[...], recv2[k].reshape(384, 512)).astype(BF)
        xs[0, k] = both[:128]
        xs[1, k] = both[128:]

    def multiply(k):
        a, h = k // 2, lax.rem(k, 2)
        for m in range(3):
            out = dot(xs[m // 2, k], fbuf[pl.ds(h * 4, 4), m].reshape(512, 512))

            @pl.when(h == 0)
            def _():
                ybuf[m, a] = out

            @pl.when(h == 1)
            def _():
                ybuf[m, a] += out

    loads[2].wait()
    loads[3].wait()
    first(0, False)
    first(1, False)
    pick2[...] = dot(perm[...], pick[...]).astype(BF)
    each(FWD - LATE, lambda k: first(k + LATE, True))
    first(2, False)
    for t in range(2):
        hit = iota((128, 384), 1) == jnp.broadcast_to(base_col + 24 * t, (128, 384))
        chose[t * 128 : (t + 1) * 128, :] = jnp.where(hit, 1.0, 0.0).astype(BF)
        hit = iota((384, 128), 0) == jnp.broadcast_to(base_row + 24 * t, (384, 128))
        chose_t[:, t * 128 : (t + 1) * 128] = jnp.where(hit, 1.0, 0.0).astype(BF)
    chose2[...] = dot(chose[...], perm[...]).astype(BF)
    chose2_t[...] = dot(perm[...], chose_t[...]).astype(BF)
    pick_t[...] = picked.T.astype(BF)
    pick2_t[...] = dot(pick_t[...], perm[...]).astype(BF)

    def forward(k):
        second(k, False)

        @pl.when(k + AHEAD < LATE)
        def _():
            first(k + AHEAD, False)

        @pl.when((k + AHEAD >= LATE) & (k + AHEAD < FWD))
        def _():
            second(k + AHEAD, True)

        @pl.when(k < 4)
        def _():
            agp_copy(k).wait_recv()

            @pl.when(k < 3)
            def _():
                agp_copy(k + 1).start()
                agm_copy(k).wait_recv()

            @pl.when(k < 2)
            def _():
                agm_copy(k + 1).start()

        @pl.when(k > 0)
        def _():
            land(k - 1, False)

        @pl.when(k == 4)
        def _():
            each(4, multiply)

        @pl.when(k == 5)
        def _():
            multiply(k - 1)

    each(LATE, forward)
    land(LATE - 1, False)
    multiply(LATE - 1)

    def finish(k):
        land(k + LATE, True)
        multiply(k + LATE)

    each(FWD - LATE, finish)

    loads[5].wait()

    def middle(block_of_rows):
        at = pl.ds(pl.multiple_of(block_of_rows * 32, 32), 32)

        def combine(m):
            outs = [None] * 4
            for a in range(4):
                for i in range(4):
                    v = ybuf[m, a, at, i * 128 : (i + 1) * 128]
                    for b in range(4):
                        term = mix[0, m, i, a, b] * v
                        outs[b] = term if outs[b] is None else outs[b] + term
            return outs

        gate = gates[at, :]
        pre_gate, pre_up, pulled = combine(0), combine(1), combine(2)
        inner = jnp.zeros((32, 128), F32)
        for b in range(4):
            s = jax.nn.sigmoid(pre_gate[b])
            act = pre_gate[b] * s
            slope = s + act * (1.0 - s)
            hidden = act * pre_up[b]
            inner = inner + hidden * pulled[b]
            back = gate * pulled[b]
            ends[0, b, at, :] = back * pre_up[b] * slope
            ends[1, b, at, :] = back * act
            ends[2, b, at, :] = gate * hidden
        ggs[at, :] = inner
        for m in range(3):
            parts = [ends[m, b, at, :] for b in range(4)]
            for a in range(4):
                for i in range(4):
                    total = mix[0, m, i, a, 0] * parts[0]
                    for b in range(1, 4):
                        total = total + mix[0, m, i, a, b] * parts[b]
                    ubuf[m, a, at, i * 128 : (i + 1) * 128] = total.astype(BF)

    each(4, middle)

    def bx_copy(k, d, early):
        o = lax.rem(g + d + 1, 8)
        src, dst = (send4, recv4) if early else (send3, recv3)
        return remote(src.at[k, o], dst.at[k, g], (bx_sem.at[0, k, d], bx_sem.at[1, k, d]), at_g(d))

    def by_copy(k, d, early):
        o = lax.rem(y + d + 1, 8)
        src, dst = (send3, recv3) if early else (send4, recv4)
        return remote(src.at[k, o], dst.at[k, y], (by_sem.at[0, k, d], by_sem.at[1, k, d]), at_y(d))

    def leave(a, early):
        both = jnp.concatenate(
            [
                dot_nt(ubuf[0, a], fbuf[4 * h : 4 * h + 4, 0].reshape(512, 512))
                + dot_nt(ubuf[1, a], fbuf[4 * h : 4 * h + 4, 1].reshape(512, 512))
                for h in range(2)
            ],
            axis=0,
        ).astype(BF)
        send3[a] = dot((chose2_t if early else chose_t)[...], both).astype(BF).reshape(8, 48, 512)
        copy, own = (by_copy, y) if early else (bx_copy, g)
        each(7, lambda d: copy(a, d, early).start())
        recv3[a, own] = send3[a, own]

    def turn(k, early):
        copy, then, own = (by_copy, bx_copy, g) if early else (bx_copy, by_copy, y)
        each(7, lambda d: copy(k, d, early).wait_recv())
        send4[k] = dot(perm[...], recv3[k].reshape(384, 512)).astype(BF).reshape(8, 48, 512)
        each(7, lambda d: then(k, d, early).start())
        recv4[k, own] = send4[k, own]

    def arrive(k, early):
        copy = bx_copy if early else by_copy
        each(7, lambda d: copy(k, d, early).wait_recv())
        both = dot((pick2_t if early else pick_t)[...], recv4[k].reshape(384, 512)).astype(BF)
        for h in range(2):
            tok_out[:, k * 1024 + h * 512 : k * 1024 + h * 512 + 512] = both[h * 128 : (h + 1) * 128]

    def part(shard, m):
        half = shard // 4
        at = pl.ds(pl.multiple_of(lax.rem(shard, 4) * 128, 128), 128)
        left = jnp.concatenate([xs[m // 2, 2 * a + half, :, at] for a in range(4)], axis=0)
        return dot_tn(left, ubuf[m].reshape(512, 512))

    def rs_copy(way, s, m):
        src, dst, sems = ((plus_s, plus_r, rsp_sem), (minus_s, minus_r, rsm_sem))[way]
        at = pl.ds(64 * way, 64) if s == 0 else pl.ds(0, 128)
        return remote(src.at[s, m, at], dst.at[s, m, at], (sems.at[0, s, m], sems.at[1, s, m]), at_z(6 * way))

    def reduce_first(m):
        far = part(lax.rem(z + 4, 8), m)
        for way, src in ((0, plus_s), (1, minus_s)):
            src[0, m, 64 * way : 64 * way + 64] = far[64 * way : 64 * way + 64].astype(BF)
            rs_copy(way, 0, m).start()

    def reduce_next(s, m):
        for way, src, got in ((0, plus_s, plus_r), (1, minus_s, minus_r)):
            own = part(lax.rem(z + 4 + (s if way else 8 - s), 8), m)
            rs_copy(way, s - 1, m).wait_recv()
            if s == 1:
                near = own[64 * way : 64 * way + 64] + got[0, m, 64 * way : 64 * way + 64].astype(F32)
                src[1, m, 64 * way : 64 * way + 64] = near.astype(BF)
                src[1, m, 64 - 64 * way : 128 - 64 * way] = own[64 - 64 * way : 128 - 64 * way].astype(BF)
            else:
                src[s, m] = (own + got[s - 1, m].astype(F32)).astype(BF)
            rs_copy(way, s, m).start()

    def reduce_last(m):
        total = part(z, m)
        rs_copy(0, 3, m).wait_recv()
        rs_copy(1, 3, m).wait_recv()
        total = total + plus_r[3, m].astype(F32) + minus_r[3, m].astype(F32)
        for i in range(4):
            fac_out[0, m, i] = total[:, i * 128 : (i + 1) * 128]

    def dots(n):
        m, a = n // 4, lax.rem(n, 4)
        for i in range(4):
            v = ybuf[m, a, :, i * 128 : (i + 1) * 128]
            for b in range(4):
                mdrow[b, pl.ds(m * 16 + i * 4 + a, 1), :] = jnp.sum(v * ends[m, b], axis=0, keepdims=True)

    def mix_copy(d):
        return remote(mixbuf.at[z], mixbuf.at[z], (mix_sem.at[0, d], mix_sem.at[1, d]), at_z(d))

    leave(0, True)
    reduce_first(0)
    reduce_first(1)
    reduce_first(2)
    leave(1, True)
    reduce_next(1, 0)
    leave(2, False)
    reduce_next(1, 1)
    reduce_next(1, 2)
    leave(3, False)
    turn(2, False)
    reduce_next(2, 0)
    turn(0, True)
    turn(3, False)
    reduce_next(2, 1)
    reduce_next(2, 2)
    arrive(0, True)
    reduce_next(3, 0)
    turn(1, True)
    reduce_next(3, 1)
    reduce_next(3, 2)

    each(12, dots)
    small = jnp.zeros((48, 128), F32)
    for b in range(4):
        small = jnp.where(iota((48, 128), 1) == b, jnp.sum(mdrow[b], axis=1, keepdims=True), small)
    mixbuf[z] = small
    each(7, lambda d: mix_copy(d).start())
    gate_col = gates[...]
    total_col = jnp.sum(ggs[...], axis=1, keepdims=True) * gate_col * (1.0 - gate_col)
    total_row = jnp.sum(jnp.where(eye, total_col, 0.0), axis=0, keepdims=True)
    gate_out[0, 0:1] = total_row[:, :64]
    gate_out[0, 1:2] = total_row[:, 64:]

    arrive(1, True)
    reduce_last(0)
    reduce_last(1)
    arrive(2, False)
    each(7, lambda d: mix_copy(d).wait_recv())
    total = mixbuf[0]
    for o in range(1, 8):
        total = total + mixbuf[o]
    for m in range(3):
        for i in range(4):
            at = (m * 4 + i) * 4
            mix_out[0, m, i] = total[at : at + 4, :4]
    reduce_last(2)
    arrive(3, False)

    each(7, lambda d: mix_copy(d).wait_send())
    each(LATE, lambda k: each(7, lambda d: (y_copy(k, d, False).wait_send(), x_copy(k, d, False).wait_send())))
    each(FWD - LATE, lambda k: each(7, lambda d: (y_copy(k + LATE, d, True).wait_send(), x_copy(k + LATE, d, True).wait_send())))
    each(EARLY, lambda k: each(7, lambda d: (bx_copy(k, d, True).wait_send(), by_copy(k, d, True).wait_send())))
    each(RET - EARLY, lambda k: each(7, lambda d: (bx_copy(k + EARLY, d, False).wait_send(), by_copy(k + EARLY, d, False).wait_send())))
    each(4, lambda s: agp_copy(s).wait_send())
    each(3, lambda s: agm_copy(s).wait_send())
    for s in range(4):
        each(3, lambda m, s=s: (rs_copy(0, s, m).wait_send(), rs_copy(1, s, m).wait_send()))


def write(*refs):
    copies = [pltpu.make_async_copy(refs[n], refs[n + 4], refs[8].at[n]) for n in range(4)]
    for copy in copies:
        copy.start()
    for copy in copies:
        copy.wait()


def shards(tokens, cotangent, factors, mix, selection, scores):
    vmem = pl.BlockSpec(memory_space=pltpu.VMEM)
    hbm = pl.BlockSpec(memory_space=pltpu.HBM)
    dma = pltpu.SemaphoreType.DMA
    row = (8, 48, 512)
    outs = (
        jax.ShapeDtypeStruct((128, 4096), BF),
        jax.ShapeDtypeStruct((1, 3, 4, 128, 128), F32),
        jax.ShapeDtypeStruct((1, 3, 4, 4, 4), F32),
        jax.ShapeDtypeStruct((1, 2, 64), F32),
    )
    results = pl.pallas_call(
        kernel,
        out_shape=outs,
        in_specs=[hbm] * 6,
        out_specs=(vmem, vmem, vmem, vmem),
        scratch_shapes=[
            *[pltpu.VMEM((128, 4096), BF)] * 2,
            pltpu.VMEM((1, 3, 4, 128, 128), BF),
            pltpu.SMEM((1, 3, 4, 4, 4), F32),
            *[pltpu.VMEM((1, 2, 64), I32)] * 2,
            pltpu.VMEM((8, 8, 128), I32),
            pltpu.VMEM((8, 8, 128), I32),
            pltpu.VMEM((384, 256), BF),
            pltpu.VMEM((256, 384), BF),
            pltpu.VMEM((256, 384), BF),
            pltpu.VMEM((384, 256), BF),
            pltpu.VMEM((384, 384), BF),
            pltpu.VMEM((384, 256), BF),
            pltpu.VMEM((256, 384), BF),
            pltpu.VMEM((256, 384), BF),
            pltpu.VMEM((384, 256), BF),
            *[pltpu.VMEM((FWD,) + row, BF)] * 4,
            *[pltpu.VMEM((RET,) + row, BF)] * 4,
            pltpu.VMEM((8, 3, 128, 512), BF),
            pltpu.VMEM((2, FWD, 128, 512), BF),
            pltpu.VMEM((3, 4, 128, 512), F32),
            pltpu.VMEM((3, 4, 128, 512), BF),
            pltpu.VMEM((3, 4, 128, 128), F32),
            pltpu.VMEM((128, 128), F32),
            pltpu.VMEM((128, 128), F32),
            pltpu.VMEM((4, 48, 128), F32),
            pltpu.VMEM((8, 48, 128), F32),
            *[pltpu.VMEM((4, 3, 128, 512), BF)] * 4,
            dma((6,)),
            dma((2, 7)),
            dma((2, 7)),
            dma((2, FWD, 7)),
            dma((2, FWD, 7)),
            dma((2, RET, 7)),
            dma((2, RET, 7)),
            dma((2, 4)),
            dma((2, 3)),
            dma((2, 4, 3)),
            dma((2, 4, 3)),
            dma((2, 7)),
        ],
        compiler_params=pltpu.CompilerParams(
            collective_id=0, has_side_effects=True, vmem_limit_bytes=46 << 20
        ),
    )(*[pltpu.with_memory_space_constraint(v, pltpu.HBM) for v in (tokens, cotangent, factors, mix, selection, scores)])
    return pl.pallas_call(
        write,
        out_shape=outs,
        in_specs=[vmem] * 4,
        out_specs=(pl.BlockSpec(memory_space=pl.ANY),) * 4,
        scratch_shapes=[dma((4,))],
    )(*[pltpu.with_memory_space_constraint(v, pltpu.VMEM) for v in results])


def solution(mesh):
    return jax.shard_map(
        shards,
        mesh=mesh,
        in_specs=(
            P(("seq", "exp"), None),
            P(("seq", "exp"), None),
            P("exp", None, None, "seq", None),
            P("exp", None, None, None, None),
            P("exp", "seq", None),
            P("exp", "seq", None),
        ),
        out_specs=(
            P(("seq", "exp"), None),
            P("exp", None, None, "seq", None),
            P("exp", None, None, None, None),
            P("exp", "seq", None),
        ),
        check_vma=False,
    )
```

```python
import jax
import jax.numpy as jnp
from jax import lax
from jax.experimental import pallas as pl
from jax.experimental.pallas import tpu as pltpu
from jax.sharding import PartitionSpec as P

MESH = pl.DeviceIdType.MESH
BF = jnp.bfloat16
F32 = jnp.float32
I32 = jnp.int32
FWD = 8
RET = 4
EARLY = 2
LATE = 6
AHEAD = 3


def dot(a, b):
    return lax.dot_general(a, b, (((1,), (0,)), ((), ())), preferred_element_type=F32)


def dot_nt(a, b):
    return lax.dot_general(a, b, (((1,), (1,)), ((), ())), preferred_element_type=F32)


def dot_tn(a, b):
    return lax.dot_general(a, b, (((0,), (0,)), ((), ())), preferred_element_type=F32)


def iota(shape, dim):
    return lax.broadcasted_iota(I32, shape, dim)


def each(n, body):
    lax.fori_loop(0, n, lambda d, carry: (body(d), carry)[1], 0)


def kernel(
    tok_in, cot_in, fac_in, mix_in, sel_in, sco_in, tok_out, fac_out, mix_out, gate_out,
    tok, cot, fac, mix, selection, scores, selx, sely, pick, pick_t, chose, chose_t, perm, pick2, pick2_t, chose2, chose2_t,
    send1, recv1, send2, recv2, send3, recv3, send4, recv4,
    fbuf, xs, ybuf, ubuf, ends, gates, ggs, mdrow, mixbuf,
    plus_s, plus_r, minus_s, minus_r,
    in_sem, selx_sem, sely_sem, y_sem, x_sem, bx_sem, by_sem, agp_sem, agm_sem, rsp_sem, rsm_sem, mix_sem,
):
    loads = [
        pltpu.make_async_copy(src, dst, in_sem.at[n])
        for n, (src, dst) in enumerate(
            ((sel_in, selection), (fac_in, fac), (tok_in, tok), (cot_in, cot), (sco_in, scores), (mix_in, mix))
        )
    ]
    for load in loads:
        load.start()
    me = lax.axis_index("exp")
    z = lax.axis_index("seq")
    core, y, x = lax.rem(me, 2), lax.rem(me // 2, 8), me // 16
    g = x * 2 + core

    def at_y(d):
        return {"exp": (x * 8 + lax.rem(y + d + 1, 8)) * 2 + core, "seq": z}

    def at_g(d):
        o = lax.rem(g + d + 1, 8)
        return {"exp": ((o // 2) * 8 + y) * 2 + lax.rem(o, 2), "seq": z}

    def at_z(d):
        return {"exp": me, "seq": lax.rem(z + d + 1, 8)}

    def remote(src, dst, sems, where):
        return pltpu.make_async_remote_copy(
            src_ref=src, dst_ref=dst, send_sem=sems[0], recv_sem=sems[1],
            device_id=where, device_id_type=MESH,
        )

    barrier = pltpu.get_barrier_semaphore()
    for place in (at_g, at_y, at_z):
        each(7, lambda d, place=place: pl.semaphore_signal(barrier, inc=1, device_id=place(d), device_id_type=MESH))
    for o in range(8):
        s = iota((48, 384), 0)
        hit = iota((48, 384), 1) == (s & 7) * 48 + (s - (s & 7)) + o
        perm[o * 48 : (o + 1) * 48, :] = jnp.where(hit, 1.0, 0.0).astype(BF)
    pl.semaphore_wait(barrier, 21)

    def selx_copy(d):
        return remote(selx.at[g], selx.at[g], (selx_sem.at[0, d], selx_sem.at[1, d]), at_g(d))

    def joined(ref):
        return jnp.concatenate([ref[0, 0:1], ref[0, 1:2]], axis=1)

    loads[0].wait()
    chosen = joined(selection)
    selx[g] = jnp.broadcast_to(chosen, (8, 128))
    each(7, lambda d: selx_copy(d).start())

    each(7, lambda d: selx_copy(d).wait())
    tile = jnp.zeros((8, 128), I32)
    for o in range(8):
        tile = jnp.where(iota((8, 128), 0) == o, selx[o], tile)
    sely[y] = tile

    def sely_copy(d):
        return remote(sely.at[y], sely.at[y], (sely_sem.at[0, d], sely_sem.at[1, d]), at_y(d))

    each(7, lambda d: sely_copy(d).start())

    loads[1].wait()
    for m in range(3):
        for i in range(4):
            fbuf[z, m, :, i * 128 : (i + 1) * 128] = fac[0, m, i]

    def agp_copy(s):
        slot = lax.rem(z - s + 8, 8)
        return remote(fbuf.at[slot], fbuf.at[slot], (agp_sem.at[0, s], agp_sem.at[1, s]), at_z(0))

    def agm_copy(s):
        slot = lax.rem(z + s, 8)
        return remote(fbuf.at[slot], fbuf.at[slot], (agm_sem.at[0, s], agm_sem.at[1, s]), at_z(6))

    agp_copy(0).start()
    agm_copy(0).start()

    eye = iota((128, 128), 0) == iota((128, 128), 1)
    lane = iota((1, 128), 1)

    def column(row):
        return jnp.sum(jnp.where(eye, jnp.broadcast_to(row, (128, 128)), 0.0), axis=1, keepdims=True)

    loads[4].wait()
    gate_row = jax.nn.sigmoid(joined(scores).astype(F32) / 64.0)
    gates[...] = jnp.broadcast_to(column(gate_row), (128, 128))
    owner = lax.shift_right_logical(chosen, 7) + jnp.where(lane >= 64, 32, 0)
    place = (lax.shift_right_logical(owner, 4) * 2 + (owner & 1)) * 48 + (lax.shift_right_logical(owner, 1) & 7)
    owner_row = owner.astype(F32)
    owner_col = column(owner_row)
    same = jnp.broadcast_to(owner_col, (128, 128)) == jnp.broadcast_to(owner_row, (128, 128))
    before = iota((128, 128), 0) < iota((128, 128), 1)
    after = iota((128, 128), 1) < iota((128, 128), 0)
    rank_row = jnp.sum(jnp.where(same & before, 1.0, 0.0), axis=0, keepdims=True)
    rank_col = jnp.sum(jnp.where(same & after, 1.0, 0.0), axis=1, keepdims=True)
    base_row = place + rank_row.astype(I32) * 8
    base_col = column(place.astype(F32)).astype(I32) + rank_col.astype(I32) * 8
    each(7, lambda d: sely_copy(d).wait())

    block, own = me // 32, lax.rem(me, 32)
    local = sely[...].reshape(64, 128) - own * 128
    wide = iota((64, 128), 1)
    valid = (local >= 0) & (local < 128) & (lax.shift_right_logical(wide, 6) == block)
    lane_f = wide.astype(F32)
    first = jnp.min(jnp.where(valid, lane_f, 999.0), axis=1, keepdims=True)
    rank = lane_f - first
    wanted = [
        jnp.sum(jnp.where(valid & (rank == float(r)), local.astype(F32) + 1000.0, 0.0), axis=1, keepdims=True) - 1000.0
        for r in range(3)
    ]
    rows = []
    for o in range(8):
        for t in range(2):
            for r in range(3):
                want = jnp.broadcast_to(wanted[r][o * 8 : (o + 1) * 8] + 128.0 * t, (8, 256))
                rows.append(jnp.where(iota((8, 256), 1).astype(F32) == want, 1.0, 0.0))
    picked = jnp.concatenate(rows, axis=0)
    pick[...] = picked.astype(BF)

    def y_copy(k, d, late):
        o = lax.rem(y + d + 1, 8)
        src, dst = (send2, recv2) if late else (send1, recv1)
        return remote(src.at[k, o], dst.at[k, y], (y_sem.at[0, k, d], y_sem.at[1, k, d]), at_y(d))

    def x_copy(k, d, late):
        o = lax.rem(g + d + 1, 8)
        src, dst = (send1, recv1) if late else (send2, recv2)
        return remote(src.at[k, o], dst.at[k, g], (x_sem.at[0, k, d], x_sem.at[1, k, d]), at_g(d))

    def first(k, late):
        cols = pl.ds(pl.multiple_of(k * 512, 512), 512)
        both = jnp.concatenate([tok[:, cols], cot[:, cols]], axis=0)
        send1[k] = dot((pick2 if late else pick)[...], both).astype(BF).reshape(8, 48, 512)
        copy, own = (x_copy, g) if late else (y_copy, y)
        each(7, lambda d: copy(k, d, late).start())
        recv1[k, own] = send1[k, own]

    def second(k, late):
        copy, then, own = (x_copy, y_copy, y) if late else (y_copy, x_copy, g)
        each(7, lambda d: copy(k, d, late).wait_recv())
        send2[k] = dot(perm[...], recv1[k].reshape(384, 512)).astype(BF).reshape(8, 48, 512)
        each(7, lambda d: then(k, d, late).start())
        recv2[k, own] = send2[k, own]

    def land(k, late):
        copy = y_copy if late else x_copy
        each(7, lambda d: copy(k, d, late).wait_recv())
        both = dot((chose2 if late else chose)[...], recv2[k].reshape(384, 512)).astype(BF)
        xs[0, k] = both[:128]
        xs[1, k] = both[128:]

    def multiply(k):
        a, h = k // 2, lax.rem(k, 2)
        for m in range(3):
            out = dot(xs[m // 2, k], fbuf[pl.ds(h * 4, 4), m].reshape(512, 512))

            @pl.when(h == 0)
            def _():
                ybuf[m, a] = out

            @pl.when(h == 1)
            def _():
                ybuf[m, a] += out

    loads[2].wait()
    loads[3].wait()
    first(0, False)
    first(1, False)
    pick2[...] = dot(perm[...], pick[...]).astype(BF)
    each(FWD - LATE, lambda k: first(k + LATE, True))
    first(2, False)
    for t in range(2):
        hit = iota((128, 384), 1) == jnp.broadcast_to(base_col + 24 * t, (128, 384))
        chose[t * 128 : (t + 1) * 128, :] = jnp.where(hit, 1.0, 0.0).astype(BF)
        hit = iota((384, 128), 0) == jnp.broadcast_to(base_row + 24 * t, (384, 128))
        chose_t[:, t * 128 : (t + 1) * 128] = jnp.where(hit, 1.0, 0.0).astype(BF)
    chose2[...] = dot(chose[...], perm[...]).astype(BF)
    chose2_t[...] = dot(perm[...], chose_t[...]).astype(BF)
    pick_t[...] = picked.T.astype(BF)
    pick2_t[...] = dot(pick_t[...], perm[...]).astype(BF)

    def forward(k):
        second(k, False)

        @pl.when(k + AHEAD < LATE)
        def _():
            first(k + AHEAD, False)

        @pl.when((k + AHEAD >= LATE) & (k + AHEAD < FWD))
        def _():
            second(k + AHEAD, True)

        @pl.when(k < 4)
        def _():
            agp_copy(k).wait_recv()

            @pl.when(k < 3)
            def _():
                agp_copy(k + 1).start()
                agm_copy(k).wait_recv()

            @pl.when(k < 2)
            def _():
                agm_copy(k + 1).start()

        @pl.when(k > 0)
        def _():
            land(k - 1, False)

        @pl.when(k == 4)
        def _():
            each(4, multiply)

        @pl.when(k == 5)
        def _():
            multiply(k - 1)

    each(LATE, forward)
    land(LATE - 1, False)
    multiply(LATE - 1)

    def finish(k):
        land(k + LATE, True)
        multiply(k + LATE)

    each(FWD - LATE, finish)

    loads[5].wait()

    def middle(block_of_rows):
        at = pl.ds(pl.multiple_of(block_of_rows * 32, 32), 32)

        def combine(m):
            outs = [None] * 4
            for a in range(4):
                for i in range(4):
                    v = ybuf[m, a, at, i * 128 : (i + 1) * 128]
                    for b in range(4):
                        term = mix[0, m, i, a, b] * v
                        outs[b] = term if outs[b] is None else outs[b] + term
            return outs

        gate = gates[at, :]
        pre_gate, pre_up, pulled = combine(0), combine(1), combine(2)
        inner = jnp.zeros((32, 128), F32)
        for b in range(4):
            s = jax.nn.sigmoid(pre_gate[b])
            act = pre_gate[b] * s
            slope = s + act * (1.0 - s)
            hidden = act * pre_up[b]
            inner = inner + hidden * pulled[b]
            back = gate * pulled[b]
            ends[0, b, at, :] = back * pre_up[b] * slope
            ends[1, b, at, :] = back * act
            ends[2, b, at, :] = gate * hidden
        ggs[at, :] = inner

    def spread(m, a):
        for at in range(0, 128, 32):
            parts = [ends[m, b, at : at + 32, :] for b in range(4)]
            for i in range(4):
                total = mix[0, m, i, a, 0] * parts[0]
                for b in range(1, 4):
                    total = total + mix[0, m, i, a, b] * parts[b]
                ubuf[m, a, at : at + 32, i * 128 : (i + 1) * 128] = total.astype(BF)

    each(4, middle)
    spread(0, 0)
    spread(1, 0)

    def bx_copy(k, d, early):
        o = lax.rem(g + d + 1, 8)
        src, dst = (send4, recv4) if early else (send3, recv3)
        return remote(src.at[k, o], dst.at[k, g], (bx_sem.at[0, k, d], bx_sem.at[1, k, d]), at_g(d))

    def by_copy(k, d, early):
        o = lax.rem(y + d + 1, 8)
        src, dst = (send3, recv3) if early else (send4, recv4)
        return remote(src.at[k, o], dst.at[k, y], (by_sem.at[0, k, d], by_sem.at[1, k, d]), at_y(d))

    def leave(a, early):
        both = jnp.concatenate(
            [
                dot_nt(ubuf[0, a], fbuf[4 * h : 4 * h + 4, 0].reshape(512, 512))
                + dot_nt(ubuf[1, a], fbuf[4 * h : 4 * h + 4, 1].reshape(512, 512))
                for h in range(2)
            ],
            axis=0,
        ).astype(BF)
        send3[a] = dot((chose2_t if early else chose_t)[...], both).astype(BF).reshape(8, 48, 512)
        copy, own = (by_copy, y) if early else (bx_copy, g)
        each(7, lambda d: copy(a, d, early).start())
        recv3[a, own] = send3[a, own]

    def turn(k, early):
        copy, then, own = (by_copy, bx_copy, g) if early else (bx_copy, by_copy, y)
        each(7, lambda d: copy(k, d, early).wait_recv())
        send4[k] = dot(perm[...], recv3[k].reshape(384, 512)).astype(BF).reshape(8, 48, 512)
        each(7, lambda d: then(k, d, early).start())
        recv4[k, own] = send4[k, own]

    def arrive(k, early):
        copy = bx_copy if early else by_copy
        each(7, lambda d: copy(k, d, early).wait_recv())
        both = dot((pick2_t if early else pick_t)[...], recv4[k].reshape(384, 512)).astype(BF)
        for h in range(2):
            tok_out[:, k * 1024 + h * 512 : k * 1024 + h * 512 + 512] = both[h * 128 : (h + 1) * 128]

    def part(shard, m):
        half = shard // 4
        at = pl.ds(pl.multiple_of(lax.rem(shard, 4) * 128, 128), 128)
        left = jnp.concatenate([xs[m // 2, 2 * a + half, :, at] for a in range(4)], axis=0)
        return dot_tn(left, ubuf[m].reshape(512, 512))

    def rs_copy(way, s, m):
        src, dst, sems = ((plus_s, plus_r, rsp_sem), (minus_s, minus_r, rsm_sem))[way]
        at = pl.ds(64 * way, 64) if s == 0 else pl.ds(0, 128)
        return remote(src.at[s, m, at], dst.at[s, m, at], (sems.at[0, s, m], sems.at[1, s, m]), at_z(6 * way))

    def reduce_first(m):
        far = part(lax.rem(z + 4, 8), m)
        for way, src in ((0, plus_s), (1, minus_s)):
            src[0, m, 64 * way : 64 * way + 64] = far[64 * way : 64 * way + 64].astype(BF)
            rs_copy(way, 0, m).start()

    def reduce_next(s, m):
        for way, src, got in ((0, plus_s, plus_r), (1, minus_s, minus_r)):
            own = part(lax.rem(z + 4 + (s if way else 8 - s), 8), m)
            rs_copy(way, s - 1, m).wait_recv()
            if s == 1:
                near = own[64 * way : 64 * way + 64] + got[0, m, 64 * way : 64 * way + 64].astype(F32)
                src[1, m, 64 * way : 64 * way + 64] = near.astype(BF)
                src[1, m, 64 - 64 * way : 128 - 64 * way] = own[64 - 64 * way : 128 - 64 * way].astype(BF)
            else:
                src[s, m] = (own + got[s - 1, m].astype(F32)).astype(BF)
            rs_copy(way, s, m).start()

    def reduce_last(m):
        total = part(z, m)
        rs_copy(0, 3, m).wait_recv()
        rs_copy(1, 3, m).wait_recv()
        total = total + plus_r[3, m].astype(F32) + minus_r[3, m].astype(F32)
        for i in range(4):
            fac_out[0, m, i] = total[:, i * 128 : (i + 1) * 128]

    def dots(n):
        m, a = n // 4, lax.rem(n, 4)
        for i in range(4):
            v = ybuf[m, a, :, i * 128 : (i + 1) * 128]
            for b in range(4):
                mdrow[b, pl.ds(m * 16 + i * 4 + a, 1), :] = jnp.sum(v * ends[m, b], axis=0, keepdims=True)

    def mix_copy(d):
        return remote(mixbuf.at[z], mixbuf.at[z], (mix_sem.at[0, d], mix_sem.at[1, d]), at_z(d))

    leave(0, True)
    each(3, lambda n: (spread(0, n + 1), spread(1, n + 1)))
    each(4, lambda n: spread(2, n))
    reduce_first(0)
    reduce_first(1)
    reduce_first(2)
    leave(1, True)
    reduce_next(1, 0)
    leave(2, False)
    reduce_next(1, 1)
    reduce_next(1, 2)
    leave(3, False)
    reduce_next(2, 0)
    turn(2, False)
    reduce_next(2, 1)
    turn(0, True)
    reduce_next(2, 2)
    turn(3, False)
    reduce_next(3, 0)
    arrive(0, True)
    turn(1, True)
    reduce_next(3, 1)
    reduce_next(3, 2)

    each(12, dots)
    small = jnp.zeros((48, 128), F32)
    for b in range(4):
        small = jnp.where(iota((48, 128), 1) == b, jnp.sum(mdrow[b], axis=1, keepdims=True), small)
    mixbuf[z] = small
    each(7, lambda d: mix_copy(d).start())
    gate_col = gates[...]
    total_col = jnp.sum(ggs[...], axis=1, keepdims=True) * gate_col * (1.0 - gate_col)
    total_row = jnp.sum(jnp.where(eye, total_col, 0.0), axis=0, keepdims=True)
    gate_out[0, 0:1] = total_row[:, :64]
    gate_out[0, 1:2] = total_row[:, 64:]

    arrive(1, True)
    reduce_last(0)
    reduce_last(1)
    reduce_last(2)
    each(7, lambda d: mix_copy(d).wait_recv())
    total = mixbuf[0]
    for o in range(1, 8):
        total = total + mixbuf[o]
    for m in range(3):
        for i in range(4):
            at = (m * 4 + i) * 4
            mix_out[0, m, i] = total[at : at + 4, :4]
    arrive(2, False)
    arrive(3, False)

    each(7, lambda d: mix_copy(d).wait_send())
    each(LATE, lambda k: each(7, lambda d: (y_copy(k, d, False).wait_send(), x_copy(k, d, False).wait_send())))
    each(FWD - LATE, lambda k: each(7, lambda d: (y_copy(k + LATE, d, True).wait_send(), x_copy(k + LATE, d, True).wait_send())))
    each(EARLY, lambda k: each(7, lambda d: (bx_copy(k, d, True).wait_send(), by_copy(k, d, True).wait_send())))
    each(RET - EARLY, lambda k: each(7, lambda d: (bx_copy(k + EARLY, d, False).wait_send(), by_copy(k + EARLY, d, False).wait_send())))
    each(4, lambda s: agp_copy(s).wait_send())
    each(3, lambda s: agm_copy(s).wait_send())
    for s in range(4):
        each(3, lambda m, s=s: (rs_copy(0, s, m).wait_send(), rs_copy(1, s, m).wait_send()))


def write(*refs):
    copies = [pltpu.make_async_copy(refs[n], refs[n + 4], refs[8].at[n]) for n in range(4)]
    for copy in copies:
        copy.start()
    for copy in copies:
        copy.wait()


def shards(tokens, cotangent, factors, mix, selection, scores):
    vmem = pl.BlockSpec(memory_space=pltpu.VMEM)
    hbm = pl.BlockSpec(memory_space=pltpu.HBM)
    dma = pltpu.SemaphoreType.DMA
    row = (8, 48, 512)
    outs = (
        jax.ShapeDtypeStruct((128, 4096), BF),
        jax.ShapeDtypeStruct((1, 3, 4, 128, 128), F32),
        jax.ShapeDtypeStruct((1, 3, 4, 4, 4), F32),
        jax.ShapeDtypeStruct((1, 2, 64), F32),
    )
    results = pl.pallas_call(
        kernel,
        out_shape=outs,
        in_specs=[hbm] * 6,
        out_specs=(vmem, vmem, vmem, vmem),
        scratch_shapes=[
            *[pltpu.VMEM((128, 4096), BF)] * 2,
            pltpu.VMEM((1, 3, 4, 128, 128), BF),
            pltpu.SMEM((1, 3, 4, 4, 4), F32),
            *[pltpu.VMEM((1, 2, 64), I32)] * 2,
            pltpu.VMEM((8, 8, 128), I32),
            pltpu.VMEM((8, 8, 128), I32),
            pltpu.VMEM((384, 256), BF),
            pltpu.VMEM((256, 384), BF),
            pltpu.VMEM((256, 384), BF),
            pltpu.VMEM((384, 256), BF),
            pltpu.VMEM((384, 384), BF),
            pltpu.VMEM((384, 256), BF),
            pltpu.VMEM((256, 384), BF),
            pltpu.VMEM((256, 384), BF),
            pltpu.VMEM((384, 256), BF),
            *[pltpu.VMEM((FWD,) + row, BF)] * 4,
            *[pltpu.VMEM((RET,) + row, BF)] * 4,
            pltpu.VMEM((8, 3, 128, 512), BF),
            pltpu.VMEM((2, FWD, 128, 512), BF),
            pltpu.VMEM((3, 4, 128, 512), F32),
            pltpu.VMEM((3, 4, 128, 512), BF),
            pltpu.VMEM((3, 4, 128, 128), F32),
            pltpu.VMEM((128, 128), F32),
            pltpu.VMEM((128, 128), F32),
            pltpu.VMEM((4, 48, 128), F32),
            pltpu.VMEM((8, 48, 128), F32),
            *[pltpu.VMEM((4, 3, 128, 512), BF)] * 4,
            dma((6,)),
            dma((2, 7)),
            dma((2, 7)),
            dma((2, FWD, 7)),
            dma((2, FWD, 7)),
            dma((2, RET, 7)),
            dma((2, RET, 7)),
            dma((2, 4)),
            dma((2, 3)),
            dma((2, 4, 3)),
            dma((2, 4, 3)),
            dma((2, 7)),
        ],
        compiler_params=pltpu.CompilerParams(
            collective_id=0, has_side_effects=True, vmem_limit_bytes=46 << 20
        ),
    )(*[pltpu.with_memory_space_constraint(v, pltpu.HBM) for v in (tokens, cotangent, factors, mix, selection, scores)])
    return pl.pallas_call(
        write,
        out_shape=outs,
        in_specs=[vmem] * 4,
        out_specs=(pl.BlockSpec(memory_space=pl.ANY),) * 4,
        scratch_shapes=[dma((4,))],
    )(*[pltpu.with_memory_space_constraint(v, pltpu.VMEM) for v in results])


def solution(mesh):
    return jax.shard_map(
        shards,
        mesh=mesh,
        in_specs=(
            P(("seq", "exp"), None),
            P(("seq", "exp"), None),
            P("exp", None, None, "seq", None),
            P("exp", None, None, None, None),
            P("exp", "seq", None),
            P("exp", "seq", None),
        ),
        out_specs=(
            P(("seq", "exp"), None),
            P("exp", None, None, "seq", None),
            P("exp", None, None, None, None),
            P("exp", "seq", None),
        ),
        check_vma=False,
    )
```
